128 devices in a mesh: seq: 32 (over y, x, core), head: 4 (over z).
Axes of the slice: x: 4, y: 4, z: 4, core: 2. Of those that a mesh axis runs over, the one named last changes fastest.
Arguments:
- queries: bfloat16 [4096, 16, 128], P('seq', 'head'), may hold values from -6 to 6
- keys: bfloat16 [4096, 16, 4, 128], P('seq', 'head'), may hold values from -6 to 6
- values: bfloat16 [4096, 16, 4, 128], P('seq', 'head'), may hold values from -6 to 6
- beta_logits: float32 [16, 4, 4096], P('head', None, 'seq'), may hold values from -10 to 4
- out_cot: bfloat16 [4096, 4096], P('seq', 'head'), may hold values from -6 to 6
- out_weight: bfloat16 [2048, 4096], P('head'), may hold values from -0.09375 to 0.09375
Outputs:
- query_grad: float32 [4096, 16, 128], P('seq', 'head')
- key_grad: float32 [4096, 16, 4, 128], P('seq', 'head')
- value_grad: float32 [4096, 16, 4, 128], P('seq', 'head')
- beta_grad: float32 [16, 4, 4096], P('head', None, 'seq')
The draws below stay inside these ranges and needn't reach their ends.
All inputs are finite; a program needn't handle non-finite values.
Results may differ from the reference program's by a relative error of at most 0.00035.
Values may be sent and summed in bfloat16 or wider, within the bound.
A program may use at most 128 MiB of HBM per device.

```python
import math
import jax
import jax.numpy as jnp
from jax import lax

D = 4096
HEAD_TOTAL = 16
HEAD_DIM = 128
REFLECTION_COUNT = 4
TOK_DEV = 128
TOKEN_TOTAL = 4096


def draw_beta_logits(key, part):
    key_sequence = jax.random.split(jax.random.fold_in(key, 17), 7)
    slow_share = 0.5
    damped_heads = jax.random.uniform(key_sequence[0], (HEAD_TOTAL,)) < slow_share
    slow_level = 0.5 * HEAD_DIM / (REFLECTION_COUNT * TOKEN_TOTAL) * jnp.exp(jax.random.uniform(key_sequence[1], (HEAD_TOTAL,), minval=math.log(0.2), maxval=0.0))
    slow_logit = jnp.log(slow_level / (2.0 - slow_level))
    fast_logit = jax.random.uniform(key_sequence[2], (HEAD_TOTAL,), minval=-1.0, maxval=1.0)
    device_factor = jax.random.uniform(key_sequence[3], (TOKEN_TOTAL // TOK_DEV,), minval=-0.7, maxval=0.7)
    per_token = jnp.repeat(device_factor, TOK_DEV)
    base_level = jnp.where(damped_heads, slow_logit, fast_logit)[:, None, None] + per_token[None, None, :]
    noise_scale = jnp.where(damped_heads, 0.7, 1.0)[:, None, None]
    logit_values = base_level + noise_scale * jax.random.normal(key_sequence[4], (HEAD_TOTAL, REFLECTION_COUNT, TOKEN_TOTAL))
    spike_position = jax.random.randint(key_sequence[5], (4,), 0, TOKEN_TOTAL)
    spike_mask = jnp.any(jnp.arange(TOKEN_TOTAL)[:, None] == spike_position[None, :], axis=1)
    spike_value = jax.random.uniform(key_sequence[6], (HEAD_TOTAL, REFLECTION_COUNT, TOKEN_TOTAL), minval=-1.5, maxval=0.5)
    logit_values = jnp.where(damped_heads[:, None, None] & spike_mask[None, None, :], spike_value, logit_values)
    return jnp.clip(logit_values, -10.0, 4.0)


def block_levels(stream_key, dims, shards, smallest, top_value):
    def one(dim, shards_of):
        heights = jax.random.uniform(jax.random.fold_in(jax.random.fold_in(stream_key, 6), dim), (shards_of,), jnp.float32, smallest / len(shards), top_value / len(shards))
        return jnp.repeat(jnp.exp(heights), dims[dim] // shards_of).reshape((-1,) + (1,) * (len(dims) - dim - 1))

    factor_of = one(*shards[0])
    for cut in shards[1:]:
        factor_of = factor_of * one(*cut)
    return factor_of


def scatter_about(stream_key, extent, scale, most, cuts=(), kind=jnp.bfloat16):
    array = scale * jax.random.normal(stream_key, extent, jnp.float32)
    if cuts:
        array = array * block_levels(stream_key, extent, cuts, -0.22, 0.18)
    return jnp.clip(array, -most, most).astype(kind)


def setup_inputs(seed: int = 0) -> dict:
    splits = jax.random.split(jax.random.key(seed), 7)
    queries = scatter_about(splits[0], (TOKEN_TOTAL, HEAD_TOTAL, HEAD_DIM), 1.0, 6.0, ((0, 32), (1, 4)))
    keys = scatter_about(splits[1], (TOKEN_TOTAL, HEAD_TOTAL, REFLECTION_COUNT, HEAD_DIM), 1.0, 6.0, ((0, 32), (1, 4)))
    values = scatter_about(splits[2], (TOKEN_TOTAL, HEAD_TOTAL, REFLECTION_COUNT, HEAD_DIM), 1.0, 6.0, ((0, 32), (1, 4)))
    beta_logits = draw_beta_logits(jax.random.fold_in(splits[6], 71), 0)
    out_cot = scatter_about(splits[4], (TOKEN_TOTAL, D), 1.0, 6.0, ((0, 32), (1, 4)))
    out_weight = scatter_about(splits[5], (HEAD_TOTAL * HEAD_DIM, D), D ** -0.5, 0.09375, ((0, 4),))
    return {"queries": queries, "keys": keys, "values": values, "beta_logits": beta_logits, "out_cot": out_cot, "out_weight": out_weight}


precise = lax.Precision.HIGHEST

def product(left, right):
    return jnp.matmul(left, right, precision=precise)

def block_maps(query_rows, key_raw, value_rows, logit_rows):
    step_count = key_raw.shape[0]
    row_count = query_rows.shape[0]
    reflections = step_count // row_count
    head_width = key_raw.shape[1]
    key_unit = key_raw * lax.rsqrt(lax.optimization_barrier(jnp.sum(key_raw * key_raw, axis=1, keepdims=True)) + 1e-06)
    beta_values = 2.0 * jax.nn.sigmoid(logit_rows)
    key_gram = product(key_unit, key_unit.T)
    lower_part = jnp.tril(key_gram, -1)
    system = jnp.eye(step_count, dtype=jnp.float32) + beta_values[:, None] * lower_part
    right_side = beta_values[:, None] * jnp.concatenate([key_unit, value_rows], axis=1)
    solved = jax.scipy.linalg.solve_triangular(system, right_side, lower=True, unit_diagonal=True)
    w_part = solved[:, :head_width]
    u_part = solved[:, head_width:]
    scaled = query_rows * head_width ** (-0.5)
    scores = product(scaled, key_unit.T)
    token_row = lax.broadcasted_iota(jnp.int32, (row_count, step_count), 0)
    step_col = lax.broadcasted_iota(jnp.int32, (row_count, step_count), 1)
    scores = jnp.where(step_col < (token_row + 1) * reflections, scores, 0.0)
    carry_map = jnp.eye(head_width, dtype=jnp.float32) - product(key_unit.T, w_part)
    offset = product(key_unit.T, u_part)
    reader = scaled - product(scores, w_part)
    direct = product(scores, u_part)
    return (carry_map, offset, reader, direct)

def block_apply(start_state, query_rows, key_raw, value_rows, logit_rows):
    carry_map, offset, reader, direct = block_maps(query_rows, key_raw, value_rows, logit_rows)
    return (product(reader, start_state) + direct, product(carry_map, start_state) + offset)

def reference(queries, keys, values, beta_logits, out_cot, out_weight):
    token_count, head_count, head_width = queries.shape
    reflections = keys.shape[2]
    out_grad = jnp.dot(out_cot.astype(jnp.float32), out_weight.T.astype(jnp.float32), preferred_element_type=jnp.float32)
    out_grad = out_grad.reshape(token_count, head_count, head_width)
    step_count = min(128, TOK_DEV * reflections)
    row_count = step_count // reflections
    block_count = token_count // row_count
    query_blocks = queries.astype(jnp.float32).reshape(block_count, row_count, head_count, head_width).transpose(0, 2, 1, 3)
    key_blocks = keys.astype(jnp.float32).reshape(block_count, row_count, head_count, reflections, head_width)
    key_blocks = key_blocks.transpose(0, 2, 1, 3, 4).reshape(block_count, head_count, step_count, head_width)
    value_blocks = values.astype(jnp.float32).reshape(block_count, row_count, head_count, reflections, head_width)
    value_blocks = value_blocks.transpose(0, 2, 1, 3, 4).reshape(block_count, head_count, step_count, head_width)
    logit_blocks = beta_logits.reshape(head_count, reflections, block_count, row_count)
    logit_blocks = logit_blocks.transpose(2, 0, 3, 1).reshape(block_count, head_count, step_count)
    grad_blocks = out_grad.reshape(block_count, row_count, head_count, head_width).transpose(0, 2, 1, 3)
    apply_heads = jax.vmap(block_apply)
    zero_state = jnp.zeros((head_count, head_width, head_width), jnp.float32)

    def advance(carried, element):
        unused, ending = apply_heads(carried, element[0], element[1], element[2], element[3])
        return (ending, carried)
    unused_end, starts = lax.scan(advance, zero_state, (query_blocks, key_blocks, value_blocks, logit_blocks))

    def retreat(adjoint, element):
        unused_out, pull_back = jax.vjp(apply_heads, element[0], element[1], element[2], element[3], element[4])
        grads = pull_back((element[5], adjoint))
        return (grads[0], grads[1:])
    unused_first, grads = lax.scan(retreat, zero_state, (starts, query_blocks, key_blocks, value_blocks, logit_blocks, grad_blocks), reverse=True)
    query_part, key_part, value_part, logit_part = grads
    query_grad = query_part.transpose(0, 2, 1, 3).reshape(token_count, head_count, head_width)
    key_grad = key_part.reshape(block_count, head_count, row_count, reflections, head_width)
    key_grad = key_grad.transpose(0, 2, 1, 3, 4).reshape(token_count, head_count, reflections, head_width)
    value_grad = value_part.reshape(block_count, head_count, row_count, reflections, head_width)
    value_grad = value_grad.transpose(0, 2, 1, 3, 4).reshape(token_count, head_count, reflections, head_width)
    beta_grad = logit_part.reshape(block_count, head_count, row_count, reflections)
    beta_grad = beta_grad.transpose(1, 3, 0, 2).reshape(head_count, reflections, token_count)
    return (query_grad, key_grad, value_grad, beta_grad)
```

```python
import jax
import jax.numpy as jnp
from jax import lax
from jax.experimental import pallas as pl
from jax.experimental.pallas import tpu as pltpu
from jax.sharding import PartitionSpec as P

F32 = jnp.float32
BF16 = jnp.bfloat16
MESH = pl.DeviceIdType.MESH
HD = 128
BLK = 128
NT = (((1,), (1,)), ((), ()))
NN = (((1,), (0,)), ((), ()))


def dg(a, b, dims):
    return lax.dot_general(a, b, dims, preferred_element_type=F32)


def split(x):
    hi = x.astype(BF16)
    lo = (x - hi.astype(F32)).astype(BF16)
    return hi, lo


def dot2(a, bs, dims=NN):
    return dg(a, bs[0], dims) + dg(a, bs[1], dims)


def dot2l(as_, b, dims=NN):
    return dg(as_[0], b, dims) + dg(as_[1], b, dims)


def dot3(as_, bs, dims=NN):
    return dg(as_[0], bs[0], dims) + (dg(as_[0], bs[1], dims) + dg(as_[1], bs[0], dims))


def iota2(shape, axis):
    return lax.broadcasted_iota(jnp.int32, shape, axis)


def to_col(row, eye):
    return jnp.sum(jnp.where(eye, row, 0.0), axis=1, keepdims=True)


def to_row(col, eye):
    return jnp.sum(jnp.where(eye, col, 0.0), axis=0, keepdims=True)


def gather_kernel(cot_ref, full_ref, send_sem, recv_sem, own_sem):
    size = lax.axis_size("head")
    me = lax.axis_index("head")
    width = cot_ref.shape[1]
    barrier = pltpu.get_barrier_semaphore()
    for step in range(1, size):
        peer = lax.rem(me + step, size)
        pl.semaphore_signal(barrier, inc=1, device_id={"head": peer}, device_id_type=MESH)
    pl.semaphore_wait(barrier, size - 1)
    columns = pl.ds(pl.multiple_of(me * width, width), width)
    copies = []
    for step in range(1, size):
        peer = lax.rem(me + step, size)
        copy = pltpu.make_async_remote_copy(
            src_ref=cot_ref,
            dst_ref=full_ref.at[:, columns],
            send_sem=send_sem.at[step],
            recv_sem=recv_sem.at[step],
            device_id={"head": peer},
            device_id_type=MESH,
        )
        copy.start()
        copies.append(copy)
    own = pltpu.make_async_copy(cot_ref, full_ref.at[:, columns], own_sem)
    own.start()
    own.wait()
    for copy in copies:
        copy.wait()


def gather_cot(cot):
    rows, width = cot.shape
    size = lax.axis_size("head")
    return pl.pallas_call(
        gather_kernel,
        out_shape=jax.ShapeDtypeStruct((rows, width * size), cot.dtype),
        in_specs=[pl.BlockSpec(memory_space=pltpu.VMEM)],
        out_specs=pl.BlockSpec(memory_space=pltpu.VMEM),
        scratch_shapes=[
            pltpu.SemaphoreType.DMA((size,)),
            pltpu.SemaphoreType.DMA((size,)),
            pltpu.SemaphoreType.DMA,
        ],
        compiler_params=pltpu.CompilerParams(collective_id=0, has_side_effects=True),
        name="gather_cot",
    )(cot)


def block_scalars(k_ref, lg_ref, b, eye):
    kb = k_ref[0, b * BLK : (b + 1) * BLK, :]
    kf = kb.astype(F32)
    rs_col = lax.rsqrt(jnp.sum(kf * kf, axis=1, keepdims=True) + 1e-06)
    beta_row = 2.0 / (1.0 + jnp.exp(-lg_ref[0, b : b + 1, :]))
    beta_col = to_col(beta_row, eye)
    return kb, kf, rs_col, beta_col


def maps_kernel(q_ref, k_ref, v_ref, lg_ref, g_ref, maps_ref, fa_ref, fb_ref, ba_ref, bb_ref):
    count = k_ref.shape[1] // BLK
    tokens = q_ref.shape[0] // count
    refl = BLK // tokens
    scale = HD ** (-0.5)
    row = iota2((BLK, BLK), 0)
    col = iota2((BLK, BLK), 1)
    eye = row == col
    eye_f = jnp.where(eye, 1.0, 0.0)
    zero = jnp.zeros((BLK, HD), F32)
    scal, lower, inv = [], [], []
    for b in range(count):
        kb, kf, rs_col, beta_col = block_scalars(k_ref, lg_ref, b, eye)
        rs_row = to_row(rs_col, eye)
        gram = dg(kb, kb, NT)
        n = jnp.where(col < row, gram * (rs_col * beta_col) * rs_row, 0.0)
        scal.append((kb, rs_col, beta_col, kb.T))
        lower.append(n)

    def level(s):
        same = (row // (2 * s)) == (col // (2 * s))
        return same & ((row // s) % 2 == 1) & ((col // s) % 2 == 0)

    mask = level(1)
    for b in range(count):
        inv.append(eye_f - jnp.where(mask, lower[b], 0.0))
    s = 2
    while s < BLK:
        mask = level(s)
        for b in range(count):
            xs = split(inv[b])
            y = dot3(xs, split(jnp.where(mask, lower[b], 0.0)))
            inv[b] = inv[b] - dot3(split(y), xs)
        s *= 2
    invs = [split(x) for x in inv]

    state = jnp.concatenate([eye_f, zero], axis=1)
    for b in range(count):
        kb, rs_col, beta_col, kt = scal[b]
        vb = v_ref[0, b * BLK : (b + 1) * BLK, :].astype(F32)
        y = jnp.concatenate([zero, vb], axis=1) - rs_col * dot2(kb, split(state))
        d = dot3(invs[b], split(beta_col * y))
        fa_ref[0, b, 0] = state[:, :HD]
        fb_ref[0, b, 0] = state[:, HD:]
        fa_ref[0, b, 1] = d[:, :HD]
        fb_ref[0, b, 1] = d[:, HD:]
        state = state + dot2(kt, split(rs_col * d))
    maps_ref[0, 0] = state[:, :HD]
    maps_ref[0, 1] = state[:, HD:]

    step_tok = iota2((BLK, tokens), 0) // refl
    tok = iota2((BLK, tokens), 1)
    seen = step_tok <= tok
    state = jnp.concatenate([eye_f, zero], axis=1)
    for b in reversed(range(count)):
        kb, rs_col, beta_col, kt = scal[b]
        qb = q_ref[b * tokens : (b + 1) * tokens, :]
        gs = split(g_ref[b * tokens : (b + 1) * tokens, :])
        sc_t = jnp.where(seen, dg(kb, qb, NT) * (rs_col * scale), 0.0)
        direct = dot3(split(sc_t), gs)
        dd = rs_col * dot2(kb, split(state)) + jnp.concatenate([zero, direct], axis=1)
        f = dot3((invs[b][0].T, invs[b][1].T), split(dd))
        ba_ref[0, b, 0] = state[:, :HD]
        bb_ref[0, b, 0] = state[:, HD:]
        ba_ref[0, b, 1] = f[:, :HD]
        bb_ref[0, b, 1] = f[:, HD:]
        source = dot2(qb.T, gs) * scale
        state = (
            state
            + jnp.concatenate([zero, source], axis=1)
            - dot2(kt, split((rs_col * beta_col) * f))
        )
    maps_ref[1, 0] = state[:, :HD]
    maps_ref[1, 1] = state[:, HD:]


def head_maps(q, k, v, lg, g):
    heads, steps, _ = k.shape
    count = steps // BLK
    rows = q.shape[0]
    saved = jax.ShapeDtypeStruct((heads, count, 2, BLK, HD), F32)
    saved_spec = pl.BlockSpec((1, count, 2, BLK, HD), lambda h: (h, 0, 0, 0, 0))
    return pl.pallas_call(
        maps_kernel,
        grid=(heads,),
        out_shape=(jax.ShapeDtypeStruct((2 * heads, 2, HD, HD), F32),) + (saved,) * 4,
        in_specs=[
            pl.BlockSpec((rows, HD), lambda h: (0, h)),
            pl.BlockSpec((1, steps, HD), lambda h: (h, 0, 0)),
            pl.BlockSpec((1, steps, HD), lambda h: (h, 0, 0)),
            pl.BlockSpec((1, count, BLK), lambda h: (h, 0, 0)),
            pl.BlockSpec((rows, HD), lambda h: (0, h)),
        ],
        out_specs=(pl.BlockSpec((2, 2, HD, HD), lambda h: (h, 0, 0, 0)),) + (saved_spec,) * 4,
        name="head_maps",
    )(q, k, v, lg, g)


def scan_kernel(maps_ref, out_ref, rbuf, pref, total, entry_in, chain_out, entries,
                send_sem, recv_sem, own_sem, chain_send, chain_recv, back_send, back_recv):
    lanes = maps_ref.shape[0]
    seq = lax.axis_size("seq")
    rows = seq // lanes
    index = lax.axis_index("seq")
    line = index // lanes
    me = lax.rem(index, lanes)
    back = lax.rem(me, 2)
    base = line * lanes
    first = back * (rows - 1)
    last = (1 - back) * (rows - 1)
    ahead = lax.rem(line + 1 - 2 * back + rows, rows)
    behind = lax.rem(line - 1 + 2 * back + rows, rows)

    barrier = pltpu.get_barrier_semaphore()
    for step in range(1, lanes):
        peer = base + lax.rem(me + step, lanes)
        pl.semaphore_signal(barrier, inc=1, device_id={"seq": peer}, device_id_type=MESH)
    for other in (ahead, behind):
        pl.semaphore_signal(
            barrier, inc=1, device_id={"seq": other * lanes + me}, device_id_type=MESH
        )
    pl.semaphore_wait(barrier, lanes + 1)

    outgoing = []
    for step in range(1, lanes):
        peer = lax.rem(me + step, lanes)
        copy = pltpu.make_async_remote_copy(
            src_ref=maps_ref.at[peer],
            dst_ref=rbuf.at[me],
            send_sem=send_sem.at[step],
            recv_sem=recv_sem.at[me],
            device_id={"seq": base + peer},
            device_id_type=MESH,
        )
        copy.start()
        outgoing.append(copy)
    own = pltpu.make_async_copy(maps_ref.at[me], rbuf.at[me], own_sem)
    own.start()

    row = iota2((HD, HD), 0)
    col = iota2((HD, HD), 1)
    total[:, :HD] = jnp.where(row == col, 1.0, 0.0)
    total[:, HD:] = jnp.zeros((HD, HD), F32)

    def advance(step, carry):
        source = step + back * (lanes - 1 - 2 * step)

        @pl.when(source == me)
        def wait_own():
            pltpu.make_async_copy(maps_ref.at[me], rbuf.at[me], own_sem).wait()

        @pl.when(source != me)
        def wait_other():
            pltpu.make_async_remote_copy(
                src_ref=maps_ref.at[source],
                dst_ref=rbuf.at[source],
                send_sem=send_sem.at[0],
                recv_sem=recv_sem.at[source],
                device_id={"seq": base + source},
                device_id_type=MESH,
            ).wait_recv()

        now = total[...]
        pref[source] = now
        moved = dot3(split(rbuf[source, 0]), split(now))
        total[:, :HD] = moved[:, :HD]
        total[:, HD:] = moved[:, HD:] + rbuf[source, 1]
        return carry

    lax.fori_loop(0, lanes, advance, 0)

    chain = pltpu.make_async_remote_copy(
        src_ref=chain_out,
        dst_ref=entry_in,
        send_sem=chain_send,
        recv_sem=chain_recv,
        device_id={"seq": ahead * lanes + me},
        device_id_type=MESH,
    )

    @pl.when(line == first)
    def start_zero():
        entry_in[...] = jnp.zeros((HD, HD), F32)

    @pl.when(line != first)
    def start_chain():
        chain.wait_recv()

    states = split(entry_in[...])

    @pl.when(line != last)
    def pass_on():
        chain_out[...] = dot3(split(total[:, :HD]), states) + total[:, HD:]
        chain.start()

    def finish(step, carry):
        entries[step] = dot3(split(pref[step, :, :HD]), states) + pref[step, :, HD:]
        return carry

    lax.fori_loop(0, lanes, finish, 0)
    returning = []
    for step in range(1, lanes):
        peer = lax.rem(me + step, lanes)
        copy = pltpu.make_async_remote_copy(
            src_ref=entries.at[peer],
            dst_ref=out_ref.at[me],
            send_sem=back_send.at[step],
            recv_sem=back_recv.at[step],
            device_id={"seq": base + peer},
            device_id_type=MESH,
        )
        copy.start()
        returning.append(copy)
    out_ref[me] = entries[me]
    for copy in outgoing:
        copy.wait_send()

    @pl.when(line != last)
    def sent_on():
        chain.wait_send()

    for copy in returning:
        copy.wait()


def scan_states(maps):
    lanes = maps.shape[0]
    return pl.pallas_call(
        scan_kernel,
        out_shape=jax.ShapeDtypeStruct((lanes, HD, HD), F32),
        in_specs=[pl.BlockSpec(memory_space=pltpu.VMEM)],
        out_specs=pl.BlockSpec(memory_space=pltpu.VMEM),
        scratch_shapes=[
            pltpu.VMEM((lanes, 2, HD, HD), F32),
            pltpu.VMEM((lanes, HD, 2 * HD), F32),
            pltpu.VMEM((HD, 2 * HD), F32),
            pltpu.VMEM((HD, HD), F32),
            pltpu.VMEM((HD, HD), F32),
            pltpu.VMEM((lanes, HD, HD), F32),
            pltpu.SemaphoreType.DMA((lanes,)),
            pltpu.SemaphoreType.DMA((lanes,)),
            pltpu.SemaphoreType.DMA,
            pltpu.SemaphoreType.DMA,
            pltpu.SemaphoreType.DMA,
            pltpu.SemaphoreType.DMA((lanes,)),
            pltpu.SemaphoreType.DMA((lanes,)),
        ],
        compiler_params=pltpu.CompilerParams(collective_id=1, has_side_effects=True),
        name="scan_states",
    )(maps)


def grads_kernel(q_ref, k_ref, lg_ref, g_ref, ent_ref, fa_ref, fb_ref, ba_ref, bb_ref,
                 qg_ref, kg_ref, vg_ref, lg_out_ref):
    count = k_ref.shape[1] // BLK
    tokens = q_ref.shape[0] // count
    refl = BLK // tokens
    scale = HD ** (-0.5)
    row = iota2((BLK, BLK), 0)
    col = iota2((BLK, BLK), 1)
    eye = row == col
    seen = (iota2((tokens, BLK), 1) // refl) <= iota2((tokens, BLK), 0)
    begin = split(ent_ref[0])
    final = split(ent_ref[1])
    for b in range(count):
        kb, kf, rs_col, beta_col = block_scalars(k_ref, lg_ref, b, eye)
        rs_row = to_row(rs_col, eye)
        s0 = dot3(split(fa_ref[0, b, 0]), begin) + fb_ref[0, b, 0]
        delta = dot3(split(fa_ref[0, b, 1]), begin) + fb_ref[0, b, 1]
        lam = dot3(split(ba_ref[0, b, 0]), final) + bb_ref[0, b, 0]
        f = dot3(split(ba_ref[0, b, 1]), final) + bb_ref[0, b, 1]
        e = beta_col * f
        dlog = jnp.sum(f * delta, axis=1, keepdims=True) * (1.0 - 0.5 * beta_col)
        lg_out_ref[0, b : b + 1, :] = to_row(dlog, eye)
        vg_ref[0, b * BLK : (b + 1) * BLK, :] = e
        qb = q_ref[b * tokens : (b + 1) * tokens, :]
        gs = split(g_ref[b * tokens : (b + 1) * tokens, :])
        ds = split(delta)
        es = split(e)
        ss = split(s0)
        ls = split(lam)
        dsc = jnp.where(seen, dot3(gs, ds, NT), 0.0)
        qg_ref[b * tokens : (b + 1) * tokens, :] = scale * (
            dot3(gs, ss, NT) + dot2l(split(dsc * rs_row), kb)
        )
        m = jnp.where(col < row, dot3(es, ds, NT), 0.0)
        sym = (m + m.T) * rs_row
        dk = (
            dot3(ds, ls, NT)
            - dot3(es, ss, NT)
            + dot2l(split(dsc.T * scale), qb)
            - dot2l(split(sym), kb)
        )
        ku = kf * rs_col
        along = jnp.sum(ku * dk, axis=1, keepdims=True)
        kg_ref[0, b * BLK : (b + 1) * BLK, :] = rs_col * (dk - ku * along)


def head_grads(q, k, lg, g, entry, saved):
    heads, steps, _ = k.shape
    count = steps // BLK
    rows = q.shape[0]
    saved_spec = pl.BlockSpec((1, count, 2, BLK, HD), lambda h: (h, 0, 0, 0, 0))
    return pl.pallas_call(
        grads_kernel,
        grid=(heads,),
        out_shape=(
            jax.ShapeDtypeStruct((rows, heads * HD), F32),
            jax.ShapeDtypeStruct((heads, steps, HD), F32),
            jax.ShapeDtypeStruct((heads, steps, HD), F32),
            jax.ShapeDtypeStruct((heads, count, BLK), F32),
        ),
        in_specs=[
            pl.BlockSpec((rows, HD), lambda h: (0, h)),
            pl.BlockSpec((1, steps, HD), lambda h: (h, 0, 0)),
            pl.BlockSpec((1, count, BLK), lambda h: (h, 0, 0)),
            pl.BlockSpec((rows, HD), lambda h: (0, h)),
            pl.BlockSpec((2, HD, HD), lambda h: (h, 0, 0)),
        ]
        + [saved_spec] * 4,
        out_specs=(
            pl.BlockSpec((rows, HD), lambda h: (0, h)),
            pl.BlockSpec((1, steps, HD), lambda h: (h, 0, 0)),
            pl.BlockSpec((1, steps, HD), lambda h: (h, 0, 0)),
            pl.BlockSpec((1, count, BLK), lambda h: (h, 0, 0)),
        ),
        name="head_grads",
    )(q, k, lg, g, entry, *saved)


def local(queries, keys, values, beta_logits, out_cot, out_weight):
    rows, heads, width = queries.shape
    refl = keys.shape[2]
    steps = rows * refl
    count = steps // BLK
    out_grad = lax.dot_general(
        gather_cot(out_cot), out_weight, NT, preferred_element_type=F32
    )
    q = queries.reshape(rows, heads * width)
    k = keys.transpose(1, 0, 2, 3).reshape(heads, steps, width)
    v = values.transpose(1, 0, 2, 3).reshape(heads, steps, width)
    lg = beta_logits.transpose(0, 2, 1).reshape(heads, count, BLK)
    maps, *saved = head_maps(q, k, v, lg, out_grad)
    entry = scan_states(maps)
    qg, kg, vg, lgg = head_grads(q, k, lg, out_grad, entry, saved)
    query_grad = qg.reshape(rows, heads, width)
    key_grad = kg.reshape(heads, rows, refl, width).transpose(1, 0, 2, 3)
    value_grad = vg.reshape(heads, rows, refl, width).transpose(1, 0, 2, 3)
    beta_grad = lgg.reshape(heads, rows, refl).transpose(0, 2, 1)
    return (query_grad, key_grad, value_grad, beta_grad)


def solution(mesh):
    return jax.shard_map(
        local,
        mesh=mesh,
        in_specs=(
            P("seq", "head", None),
            P("seq", "head", None, None),
            P("seq", "head", None, None),
            P("head", None, "seq"),
            P("seq", "head"),
            P("head", None),
        ),
        out_specs=(
            P("seq", "head", None),
            P("seq", "head", None, None),
            P("seq", "head", None, None),
            P("head", None, "seq"),
        ),
        check_vma=False,
    )
```

```python
import jax
import jax.numpy as jnp
from jax import lax
from jax.experimental import pallas as pl
from jax.experimental.pallas import tpu as pltpu
from jax.sharding import PartitionSpec as P

F32 = jnp.float32
BF16 = jnp.bfloat16
MESH = pl.DeviceIdType.MESH
HD = 128
BLK = 128
NT = (((1,), (1,)), ((), ()))
NN = (((1,), (0,)), ((), ()))


def dg(a, b, dims):
    return lax.dot_general(a, b, dims, preferred_element_type=F32)


def split(x):
    hi = x.astype(BF16)
    lo = (x - hi.astype(F32)).astype(BF16)
    return hi, lo


def dot2(a, bs):
    return dg(jnp.concatenate([a, a], 1), jnp.concatenate(bs, 0), NN)


def dot2l(as_, b):
    return dg(jnp.concatenate(as_, 1), jnp.concatenate([b, b], 0), NN)


def dot3(as_, bs):
    left = jnp.concatenate([as_[0], as_[1], as_[0]], 1)
    right = jnp.concatenate([bs[0], bs[0], bs[1]], 0)
    return dg(left, right, NN)


def dot3t(as_, bs):
    left = jnp.concatenate([as_[0], as_[1], as_[0]], 1)
    right = jnp.concatenate([bs[0], bs[0], bs[1]], 1)
    return dg(left, right, NT)


def iota2(shape, axis):
    return lax.broadcasted_iota(jnp.int32, shape, axis)


def to_row(full, eye):
    return jnp.sum(jnp.where(eye, full, 0.0), axis=0, keepdims=True)


def layer_kernel(q_ref, k_ref, v_ref, lg_ref, cot_ref, w_ref,
                 qg_ref, kg_ref, vg_ref, lgg_ref,
                 wide, kh, ktr, vh, qh, rsf, btf, invt, gsp, fa, fb, ba, bb,
                 full, wbuf, maps, rbuf, pref, total, entry_in, chain_out, entries, backs,
                 w_sem, cot_own, cot_send, cot_recv, send_sem, recv_sem, own_sem,
                 chain_send, chain_recv, back_send, back_recv):
    heads, refl, rows = lg_ref.shape
    steps = rows * refl
    count = steps // BLK
    tokens = rows // count
    scale = HD ** (-0.5)
    lanes = 2 * heads
    zsize = lax.axis_size("head")
    seq = lax.axis_size("seq")
    lines = seq // lanes
    zme = lax.axis_index("head")
    index = lax.axis_index("seq")
    line = index // lanes
    me = lax.rem(index, lanes)
    back = lax.rem(me, 2)
    home = me // 2
    base = line * lanes
    first = back * (lines - 1)
    last = (1 - back) * (lines - 1)
    ahead = lax.rem(line + 1 - 2 * back + lines, lines)
    behind = lax.rem(line - 1 + 2 * back + lines, lines)

    fetch_w = pltpu.make_async_copy(w_ref, wbuf, w_sem)
    fetch_w.start()
    barrier = pltpu.get_barrier_semaphore()
    for step in range(1, zsize):
        peer = lax.rem(zme + step, zsize)
        pl.semaphore_signal(barrier, inc=1, device_id={"head": peer}, device_id_type=MESH)
    for step in range(1, lanes):
        peer = base + lax.rem(me + step, lanes)
        pl.semaphore_signal(barrier, inc=1, device_id={"seq": peer}, device_id_type=MESH)
    for other in (ahead, behind):
        pl.semaphore_signal(
            barrier, inc=1, device_id={"seq": other * lanes + me}, device_id_type=MESH
        )

    per_token = heads * refl
    wide[...] = k_ref[...].astype(F32)
    for h in range(heads):
        for r in range(refl):
            kh[h, pl.ds(r, rows, stride=refl), :] = wide[
                pl.ds(h * refl + r, rows, stride=per_token), :
            ]
    wide[...] = v_ref[...].astype(F32)
    for h in range(heads):
        for r in range(refl):
            vh[h, pl.ds(r, rows, stride=refl), :] = wide[
                pl.ds(h * refl + r, rows, stride=per_token), :
            ]
    wide[pl.ds(0, rows * heads), :] = q_ref[...].astype(F32)
    for h in range(heads):
        qh[h] = wide[pl.ds(h, rows, stride=heads), :].astype(BF16)

    pl.semaphore_wait(barrier, zsize + lanes)

    cot_copies = []
    for step in range(1, zsize):
        copy = pltpu.make_async_remote_copy(
            src_ref=cot_ref,
            dst_ref=full.at[zme],
            send_sem=cot_send.at[step],
            recv_sem=cot_recv.at[step],
            device_id={"head": lax.rem(zme + step, zsize)},
            device_id_type=MESH,
        )
        copy.start()
        cot_copies.append(copy)
    own_cot = pltpu.make_async_copy(cot_ref, full.at[zme], cot_own)
    own_cot.start()

    row = iota2((BLK, BLK), 0)
    col = iota2((BLK, BLK), 1)
    eye = row == col
    eye_f = jnp.where(eye, 1.0, 0.0)
    zero = jnp.zeros((BLK, HD), F32)

    def level(s):
        same = (row // (2 * s)) == (col // (2 * s))
        return same & ((row // s) % 2 == 1) & ((col // s) % 2 == 0)

    def post(peer):
        @pl.when(peer != me)
        def post_other():
            pltpu.make_async_remote_copy(
                src_ref=maps.at[peer],
                dst_ref=rbuf.at[me],
                send_sem=send_sem.at[peer],
                recv_sem=recv_sem.at[me],
                device_id={"seq": base + peer},
                device_id_type=MESH,
            ).start()

        @pl.when(peer == me)
        def post_own():
            pltpu.make_async_copy(maps.at[peer], rbuf.at[peer], own_sem).start()

    def forward(turn, carry):
        pair = (lax.rem(home + 2 + turn, heads), lax.rem(home + 1 - turn, heads))
        units = [(h, b) for b in range(count) for h in pair]
        lower, inv = [], []
        for h, b in units:
            span = pl.ds(b * BLK, BLK)
            kf = kh[h, span, :]
            kb = kf.astype(BF16)
            rs = lax.rsqrt(jnp.sum(kf * kf, axis=1, keepdims=True) + 1e-06)
            beta4 = 2.0 / (1.0 + jnp.exp(-lg_ref[h]))
            beta_all = jnp.tile(jnp.concatenate([beta4] * (8 // refl), 0), (BLK // 8, 1))
            beta = jnp.sum(
                jnp.where(col == row // refl + b * tokens, beta_all, 0.0), axis=1, keepdims=True
            )
            rs = jnp.broadcast_to(rs, (BLK, HD))
            beta = jnp.broadcast_to(beta, (BLK, HD))
            rsf[h, span, :] = rs
            btf[h, span, :] = beta
            ktr[h, b] = kb.T
            n = jnp.where(col < row, dg(kb, kb, NT) * (rs * beta) * to_row(rs, eye), 0.0)
            lower.append(n)
        mask = level(1)
        for n in lower:
            inv.append(eye_f - jnp.where(mask, n, 0.0))
        s = 2
        while s < BLK:
            mask = level(s)
            for i, n in enumerate(lower):
                xs = split(inv[i])
                y = dot3(xs, split(jnp.where(mask, n, 0.0)))
                inv[i] = inv[i] - dot3(split(y), xs)
            s *= 2
        invs = [split(x) for x in inv]
        for (h, b), x in zip(units, invs):
            invt[h, b, 0] = x[0].T
            invt[h, b, 1] = x[1].T
        state = [jnp.concatenate([eye_f, zero], axis=1) for h in pair]
        for b in range(count):
            span = pl.ds(b * BLK, BLK)
            for i, h in enumerate(pair):
                now = state[i]
                kb = kh[h, span, :].astype(BF16)
                rs = rsf[h, span, :]
                beta = btf[h, span, :]
                moved = dot2(kb, split(now))
                y = jnp.concatenate(
                    [(-rs * beta) * moved[:, :HD], beta * (vh[h, span, :] - rs * moved[:, HD:])],
                    axis=1,
                )
                d = dot3(invs[b * len(pair) + i], split(y))
                fa[h, b, 0] = now[:, :HD]
                fb[h, b, 0] = now[:, HD:]
                fa[h, b, 1] = d[:, :HD]
                fb[h, b, 1] = d[:, HD:]
                rs2 = jnp.concatenate([rs, rs], axis=1)
                state[i] = now + dot2(ktr[h, b], split(rs2 * d))
        for i, h in enumerate(pair):
            maps[2 * h, 0] = state[i][:, :HD]
            maps[2 * h, 1] = state[i][:, HD:]
        for h in pair:
            post(2 * h)
        return carry

    lax.fori_loop(0, heads // 2, forward, 0)

    own_cot.wait()
    for copy in cot_copies:
        copy.wait()
    fetch_w.wait()
    width = cot_ref.shape[1]
    for n in range(heads // 2):
        acc = jnp.zeros((rows, 2 * HD), F32)
        for j in range(zsize):
            acc = acc + dg(
                full[j],
                wbuf[2 * n * HD : 2 * (n + 1) * HD, j * width : (j + 1) * width],
                NT,
            )
        for i in range(2):
            hi, lo = split(acc[:, i * HD : (i + 1) * HD])
            gsp[2 * n + i, 0] = hi
            gsp[2 * n + i, 1] = lo

    seen_t = (iota2((BLK, tokens), 0) // refl) <= iota2((BLK, tokens), 1)

    def backward(turn, carry):
        pair = (lax.rem(home + 2 + turn, heads), lax.rem(home + 1 - turn, heads))
        state = [jnp.concatenate([eye_f, zero], axis=1) for h in pair]
        for b in reversed(range(count)):
            span = pl.ds(b * BLK, BLK)
            tspan = pl.ds(b * tokens, tokens)
            for i, h in enumerate(pair):
                now = state[i]
                kb = kh[h, span, :].astype(BF16)
                rs = rsf[h, span, :]
                beta = btf[h, span, :]
                qb = qh[h, tspan, :]
                gs = (gsp[h, 0, tspan, :], gsp[h, 1, tspan, :])
                sc_t = jnp.where(seen_t, dg(kb, qb, NT) * (rs[:, :tokens] * scale), 0.0)
                direct = dot3(split(sc_t), gs)
                moved = dot2(kb, split(now))
                dd = jnp.concatenate([rs * moved[:, :HD], rs * moved[:, HD:] + direct], axis=1)
                f = dot3((invt[h, b, 0], invt[h, b, 1]), split(dd))
                ba[h, b, 0] = now[:, :HD]
                bb[h, b, 0] = now[:, HD:]
                ba[h, b, 1] = f[:, :HD]
                bb[h, b, 1] = f[:, HD:]
                source = dot2(qb.T, gs) * scale
                rb = rs * beta
                rb2 = jnp.concatenate([rb, rb], axis=1)
                state[i] = (
                    now
                    + jnp.concatenate([zero, source], axis=1)
                    - dot2(ktr[h, b], split(rb2 * f))
                )
        for i, h in enumerate(pair):
            maps[2 * h + 1, 0] = state[i][:, :HD]
            maps[2 * h + 1, 1] = state[i][:, HD:]
        for h in pair:
            post(2 * h + 1)
        return carry

    lax.fori_loop(0, heads // 2, backward, 0)

    total[:, :HD] = eye_f
    total[:, HD:] = zero

    def advance(step, carry):
        source = step + back * (lanes - 1 - 2 * step)

        @pl.when(source == me)
        def wait_own():
            pltpu.make_async_copy(maps.at[me], rbuf.at[me], own_sem).wait()

        @pl.when(source != me)
        def wait_other():
            pltpu.make_async_remote_copy(
                src_ref=maps.at[source],
                dst_ref=rbuf.at[source],
                send_sem=send_sem.at[source],
                recv_sem=recv_sem.at[source],
                device_id={"seq": base + source},
                device_id_type=MESH,
            ).wait_recv()

        now = total[...]
        pref[source] = now
        moved = dot3(split(rbuf[source, 0]), split(now))
        total[:, :HD] = moved[:, :HD]
        total[:, HD:] = moved[:, HD:] + rbuf[source, 1]
        return carry

    lax.fori_loop(0, lanes, advance, 0)

    chain = pltpu.make_async_remote_copy(
        src_ref=chain_out,
        dst_ref=entry_in,
        send_sem=chain_send,
        recv_sem=chain_recv,
        device_id={"seq": ahead * lanes + me},
        device_id_type=MESH,
    )

    @pl.when(line == first)
    def start_zero():
        entry_in[...] = jnp.zeros((HD, HD), F32)

    @pl.when(line != first)
    def start_chain():
        chain.wait_recv()

    states = split(entry_in[...])

    @pl.when(line != last)
    def pass_on():
        chain_out[...] = dot3(split(total[:, :HD]), states) + total[:, HD:]
        chain.start()

    def give(peer):
        return pltpu.make_async_remote_copy(
            src_ref=entries.at[peer],
            dst_ref=backs.at[me],
            send_sem=back_send.at[peer],
            recv_sem=back_recv.at[me],
            device_id={"seq": base + peer},
            device_id_type=MESH,
        )

    def finish(step, carry):
        peer = lax.rem(me + step, lanes)
        entries[peer] = dot3(split(pref[peer, :, :HD]), states) + pref[peer, :, HD:]
        give(peer).start()
        return carry

    lax.fori_loop(1, lanes, finish, 0)
    backs[me] = dot3(split(pref[me, :, :HD]), states) + pref[me, :, HD:]

    seen = (iota2((tokens, BLK), 1) // refl) <= iota2((tokens, BLK), 0)

    def take(source):
        @pl.when(source != me)
        def take_other():
            pltpu.make_async_remote_copy(
                src_ref=entries.at[source],
                dst_ref=backs.at[source],
                send_sem=back_send.at[source],
                recv_sem=back_recv.at[source],
                device_id={"seq": base + source},
                device_id_type=MESH,
            ).wait_recv()

    def grads(turn, carry):
        offset = turn + (turn // 2) * (1 - 2 * lax.rem(turn, 2))
        h = lax.rem(home + offset, heads)
        take(2 * h)
        take(2 * h + 1)
        begin = split(backs[2 * h])
        final = split(backs[2 * h + 1])
        acc = jnp.zeros((8, rows), F32)
        for b in range(count):
            span = pl.ds(b * BLK, BLK)
            tspan = pl.ds(b * tokens, tokens)
            kf = kh[h, span, :]
            kb = kf.astype(BF16)
            rs = rsf[h, span, :]
            beta = btf[h, span, :]
            rs_row = to_row(rs, eye)
            s0 = dot3(split(fa[h, b, 0]), begin) + fb[h, b, 0]
            delta = dot3(split(fa[h, b, 1]), begin) + fb[h, b, 1]
            lam = dot3(split(ba[h, b, 0]), final) + bb[h, b, 0]
            f = dot3(split(ba[h, b, 1]), final) + bb[h, b, 1]
            e = beta * f
            dlog = jnp.sum(f * delta, axis=1, keepdims=True) * (1.0 - 0.5 * beta)
            dlog = jnp.where(col == row // refl + b * tokens, dlog, 0.0)
            for i in range(BLK // 8):
                acc = acc + dlog[8 * i : 8 * (i + 1), :]
            vg_ref[h, span, :] = e
            qb = qh[h, tspan, :]
            gs = (gsp[h, 0, tspan, :], gsp[h, 1, tspan, :])
            ds, es, ss, ls = split(delta), split(e), split(s0), split(lam)
            dsc = jnp.where(seen, dot3t(gs, ds), 0.0)
            qg_ref[h, tspan, :] = scale * (dot3t(gs, ss) + dot2l(split(dsc * rs_row), kb))
            m = jnp.where(col < row, dot3t(es, ds), 0.0)
            sym = (m + m.T) * rs_row
            dk = (
                dot3t(ds, ls)
                - dot3t(es, ss)
                + dot2l(split(dsc.T * scale), qb)
                - dot2l(split(sym), kb)
            )
            ku = kf * rs
            along = jnp.sum(ku * dk, axis=1, keepdims=True)
            kg_ref[h, span, :] = rs * (dk - ku * along)
        out = acc[:refl]
        for i in range(1, 8 // refl):
            out = out + acc[i * refl : (i + 1) * refl]
        lgg_ref[h] = out
        return carry

    lax.fori_loop(0, heads, grads, 0)

    def drain(step, carry):
        peer = lax.rem(me + step, lanes)
        pltpu.make_async_remote_copy(
            src_ref=maps.at[peer],
            dst_ref=rbuf.at[me],
            send_sem=send_sem.at[peer],
            recv_sem=recv_sem.at[me],
            device_id={"seq": base + peer},
            device_id_type=MESH,
        ).wait_send()
        give(peer).wait_send()
        return carry

    lax.fori_loop(1, lanes, drain, 0)

    @pl.when(line != last)
    def sent_on():
        chain.wait_send()


def layer(q, k, v, lg, cot, w):
    heads, refl, rows = lg.shape
    steps = rows * refl
    count = steps // BLK
    lanes = 2 * heads
    zsize = lax.axis_size("head")
    dma = pltpu.SemaphoreType.DMA
    vm = pl.BlockSpec(memory_space=pltpu.VMEM)
    saved = pltpu.VMEM((heads, count, 2, BLK, HD), F32)
    return pl.pallas_call(
        layer_kernel,
        out_shape=(
            jax.ShapeDtypeStruct((heads, rows, HD), F32),
            jax.ShapeDtypeStruct((heads, steps, HD), F32),
            jax.ShapeDtypeStruct((heads, steps, HD), F32),
            jax.ShapeDtypeStruct(lg.shape, F32),
        ),
        in_specs=[vm] * 5 + [pl.BlockSpec(memory_space=pl.ANY)],
        out_specs=(vm,) * 4,
        scratch_shapes=[
            pltpu.VMEM((rows * heads * refl, HD), F32),
            pltpu.VMEM((heads, steps, HD), F32),
            pltpu.VMEM((heads, count, HD, BLK), BF16),
            pltpu.VMEM((heads, steps, HD), F32),
            pltpu.VMEM((heads, rows, HD), BF16),
            pltpu.VMEM((heads, steps, HD), F32),
            pltpu.VMEM((heads, steps, HD), F32),
            pltpu.VMEM((heads, count, 2, BLK, BLK), BF16),
            pltpu.VMEM((heads, 2, rows, HD), BF16),
            saved, saved, saved, saved,
            pltpu.VMEM((zsize,) + cot.shape, BF16),
            pltpu.VMEM(w.shape, BF16),
            pltpu.VMEM((lanes, 2, HD, HD), F32),
            pltpu.VMEM((lanes, 2, HD, HD), F32),
            pltpu.VMEM((lanes, HD, 2 * HD), F32),
            pltpu.VMEM((HD, 2 * HD), F32),
            pltpu.VMEM((HD, HD), F32),
            pltpu.VMEM((HD, HD), F32),
            pltpu.VMEM((lanes, HD, HD), F32),
            pltpu.VMEM((lanes, HD, HD), F32),
            dma, dma, dma((zsize,)), dma((zsize,)),
            dma((lanes,)), dma((lanes,)), dma,
            dma, dma, dma((lanes,)), dma((lanes,)),
        ],
        compiler_params=pltpu.CompilerParams(collective_id=0, has_side_effects=True),
        name="layer",
    )(q, k, v, lg, cot, w)


def local(queries, keys, values, beta_logits, out_cot, out_weight):
    rows, heads, width = queries.shape
    refl = keys.shape[2]
    qg, kg, vg, lgg = layer(
        queries.reshape(rows * heads, width),
        keys.reshape(rows * heads * refl, width),
        values.reshape(rows * heads * refl, width),
        beta_logits,
        out_cot,
        out_weight,
    )
    query_grad = qg.transpose(1, 0, 2)
    key_grad = kg.reshape(heads, rows, refl, width).transpose(1, 0, 2, 3)
    value_grad = vg.reshape(heads, rows, refl, width).transpose(1, 0, 2, 3)
    return (query_grad, key_grad, value_grad, lgg)


def solution(mesh):
    return jax.shard_map(
        local,
        mesh=mesh,
        in_specs=(
            P("seq", "head", None),
            P("seq", "head", None, None),
            P("seq", "head", None, None),
            P("head", None, "seq"),
            P("seq", "head"),
            P("head", None),
        ),
        out_specs=(
            P("seq", "head", None),
            P("seq", "head", None, None),
            P("seq", "head", None, None),
            P("head", None, "seq"),
        ),
        check_vma=False,
    )
```

```python
import jax
import jax.numpy as jnp
from jax import lax
from jax.experimental import pallas as pl
from jax.experimental.pallas import tpu as pltpu
from jax.sharding import PartitionSpec as P

F32 = jnp.float32
BF16 = jnp.bfloat16
MESH = pl.DeviceIdType.MESH
HD = 128
BLK = 128
NT = (((1,), (1,)), ((), ()))
NN = (((1,), (0,)), ((), ()))


def dg(a, b, dims):
    return lax.dot_general(a, b, dims, preferred_element_type=F32)


def split(x):
    hi = x.astype(BF16)
    lo = (x - hi.astype(F32)).astype(BF16)
    return hi, lo


def dot2(a, bs):
    return dg(jnp.concatenate([a, a], 1), jnp.concatenate(bs, 0), NN)


def dot2l(as_, b):
    return dg(jnp.concatenate(as_, 1), jnp.concatenate([b, b], 0), NN)


def dot3(as_, bs):
    left = jnp.concatenate([as_[0], as_[1], as_[0]], 1)
    right = jnp.concatenate([bs[0], bs[0], bs[1]], 0)
    return dg(left, right, NN)


def dot3t(as_, bs):
    left = jnp.concatenate([as_[0], as_[1], as_[0]], 1)
    right = jnp.concatenate([bs[0], bs[0], bs[1]], 1)
    return dg(left, right, NT)


def iota2(shape, axis):
    return lax.broadcasted_iota(jnp.int32, shape, axis)


def to_row(full, eye):
    return jnp.sum(jnp.where(eye, full, 0.0), axis=0, keepdims=True)


def remote(src, dst, send, recv, **device):
    return pltpu.make_async_remote_copy(
        src_ref=src,
        dst_ref=dst,
        send_sem=send,
        recv_sem=recv,
        device_id=device,
        device_id_type=MESH,
    )


def diagonal_inverse(lower, small, row, col, spread):
    units = len(lower)
    packed = []
    band = col[:small] // small
    for n in lower:
        acc = jnp.where(band == 0, n[:small], 0.0)
        for i in range(1, BLK // small):
            acc = jnp.where(band == i, n[i * small : (i + 1) * small], acc)
        packed.append(acc)
    hi, lo = split(jnp.concatenate(packed, 0))
    both = jnp.concatenate([hi, lo], 1)
    unit = jnp.where(row[:small] == col[:small] % small, 1.0, 0.0)
    xs = [unit] * units
    for j in range(small - 1):
        factor = dg(both, spread[j], NN)
        for u in range(units):
            xs[u] = xs[u] - factor[u * small : (u + 1) * small] * xs[u][j : j + 1]
    return [
        jnp.concatenate([jnp.where(band == i, x, 0.0) for i in range(BLK // small)], 0)
        for x in xs
    ]


def grow_inverse(inv, lower, s, row, col):
    mask = ((row // (2 * s)) == (col // (2 * s))) & ((col // s) % 2 == 0)
    odds = [slice(i, i + s) for i in range(s, BLK, 2 * s)]
    grown = []
    for x, n in zip(inv, lower):
        cut = jnp.where(mask, n, 0.0)
        below = jnp.concatenate([cut[o] for o in odds], 0)
        y = dot3(split(below), split(x))
        gap = jnp.zeros((s, BLK), F32)
        parts = []
        for i in range(len(odds)):
            parts += [gap, y[i * s : (i + 1) * s]]
        odd = jnp.concatenate([x[o] for o in odds], 0)
        new = odd - dot3(split(odd), split(jnp.concatenate(parts, 0)))
        parts = []
        for i, o in enumerate(odds):
            parts += [x[o.start - s : o.start], new[i * s : (i + 1) * s]]
        grown.append(jnp.concatenate(parts, 0))
    return grown


def layer_kernel(q_ref, k_ref, v_ref, lg_ref, cot_ref, w_ref,
                 qg_ref, kg_ref, vg_ref, lgg_ref,
                 wide, kh, ktr, vh, qh, rsf, btf, invn, invt, gsp, fa, fb, ba, bb,
                 full, wbuf, mine, pm, comp, rbuf, pref, total, entry_in, ahead_map, chain_out,
                 entries, both,
                 w_sem, cot_own, cot_send, cot_recv, pm_send, pm_recv, comp_send, comp_recv,
                 chain_send, chain_recv, map_recv, ent_send, ent_recv, oth_send, oth_recv):
    heads, refl, rows = lg_ref.shape
    steps = rows * refl
    count = steps // BLK
    tokens = rows // count
    scale = HD ** (-0.5)
    lanes = 2 * heads
    zsize = lax.axis_size("head")
    lines = lax.axis_size("seq") // lanes
    zme = lax.axis_index("head")
    index = lax.axis_index("seq")
    line = index // lanes
    me = lax.rem(index, lanes)
    back = lax.rem(me, 2)
    home = me // 2
    partner = index + 1 - 2 * back
    rank = line + back * (lines - 1 - 2 * line)

    def chip(x):
        return line * lanes + 2 * x + back

    def at_rank(r):
        return (r + back * (lines - 1 - 2 * r)) * lanes + me

    fetch_w = pltpu.make_async_copy(w_ref, wbuf, w_sem)
    fetch_w.start()
    barrier = pltpu.get_barrier_semaphore()
    zright = lax.rem(zme + 1, zsize)
    zleft = lax.rem(zme + zsize - 1, zsize)
    for peer in (zright, zleft):
        pl.semaphore_signal(barrier, inc=1, device_id={"head": peer}, device_id_type=MESH)
    friends = [partner]
    friends += [chip(lax.rem(home + step, heads)) for step in range(1, heads)]
    friends += [lax.rem(line + step, lines) * lanes + me for step in range(1, lines)]
    for peer in friends:
        pl.semaphore_signal(barrier, inc=1, device_id={"seq": peer}, device_id_type=MESH)

    per_token = heads * refl
    wide[...] = k_ref[...].astype(F32)
    for h in range(heads):
        for r in range(refl):
            kh[h, pl.ds(r, rows, stride=refl), :] = wide[
                pl.ds(h * refl + r, rows, stride=per_token), :
            ]

    half = rows // 2
    low, high = pl.ds(0, half), pl.ds(half, half)
    cot_copies = [
        remote(cot_ref.at[low], full.at[zme, low], cot_send.at[0], cot_recv.at[0], head=zright),
        remote(cot_ref.at[high], full.at[zme, high], cot_send.at[1], cot_recv.at[1], head=zleft),
        remote(cot_ref.at[high], full.at[zme, high], cot_send.at[2], cot_recv.at[2], head=zright),
        remote(cot_ref.at[low], full.at[zme, low], cot_send.at[3], cot_recv.at[3], head=zleft),
    ]
    own_cot = pltpu.make_async_copy(cot_ref, full.at[zme], cot_own)
    own_cot.start()
    hand_right = remote(
        full.at[zleft, low], full.at[zleft, low], cot_send.at[4], cot_recv.at[4], head=zright
    )
    hand_left = remote(
        full.at[zright, high], full.at[zright, high], cot_send.at[5], cot_recv.at[5], head=zleft
    )

    wide[...] = v_ref[...].astype(F32)
    for h in range(heads):
        for r in range(refl):
            vh[h, pl.ds(r, rows, stride=refl), :] = wide[
                pl.ds(h * refl + r, rows, stride=per_token), :
            ]
    wide[pl.ds(0, rows * heads), :] = q_ref[...].astype(F32)
    for h in range(heads):
        qh[h] = wide[pl.ds(h, rows, stride=heads), :].astype(BF16)

    row = iota2((BLK, BLK), 0)
    col = iota2((BLK, BLK), 1)
    eye = row == col
    eye_f = jnp.where(eye, 1.0, 0.0)
    zero = jnp.zeros((BLK, HD), F32)
    small = 16

    def invert(turn, carry):
        @pl.when(turn == 1)
        def greet():
            pl.semaphore_wait(barrier, 2 + len(friends))
            for copy in cot_copies:
                copy.start()

        units = [(2 * turn + i, b) for b in range(count) for i in range(2)]
        lower = []
        for h, b in units:
            span = pl.ds(b * BLK, BLK)
            kf = kh[h, span, :]
            kb = kf.astype(BF16)
            rs = lax.rsqrt(jnp.sum(kf * kf, axis=1, keepdims=True) + 1e-06)
            beta4 = 2.0 / (1.0 + jnp.exp(-lg_ref[h]))
            beta_all = jnp.tile(jnp.concatenate([beta4] * (8 // refl), 0), (BLK // 8, 1))
            beta = jnp.sum(
                jnp.where(col == row // refl + b * tokens, beta_all, 0.0), axis=1, keepdims=True
            )
            rs = jnp.broadcast_to(rs, (BLK, HD))
            beta = jnp.broadcast_to(beta, (BLK, HD))
            rsf[h, span, :] = rs
            btf[h, span, :] = beta
            ktr[h, b] = kb.T
            n = jnp.where(col < row, dg(kb, kb, NT) * (rs * beta) * to_row(rs, eye), 0.0)
            lower.append(n)
        spread = []
        for j in range(small - 1):
            pick = jnp.where(row == (col // small) * small + j, 1.0, 0.0).astype(BF16)
            spread.append(jnp.concatenate([pick, pick], 0))
        inv = diagonal_inverse(lower, small, row, col, spread)
        s = small
        while s < BLK:
            inv = grow_inverse(inv, lower, s, row, col)
            s *= 2
        for (h, b), x in zip(units, inv):
            hi, lo = split(x)
            invn[h, b, 0] = hi
            invn[h, b, 1] = lo
            invt[h, b, 0] = hi.T
            invt[h, b, 1] = lo.T
        return carry

    lax.fori_loop(0, heads // 2, invert, 0)
    cot_copies[0].wait_recv()
    hand_right.start()
    cot_copies[1].wait_recv()
    hand_left.start()

    def hand_over(direction, h):
        return remote(mine.at[direction, h], pm.at[h], pm_send.at[h], pm_recv.at[h], seq=partner)

    def post(h):
        return remote(
            comp.at[h], rbuf.at[home], comp_send.at[h], comp_recv.at[home], seq=chip(h)
        )

    def combine(direction, h):
        hand_over(direction, h).wait_recv()
        moved = dot3(split(pm[h, :, :HD]), split(mine[direction, h]))
        moved = jnp.concatenate([moved[:, :HD], moved[:, HD:] + pm[h, :, HD:]], axis=1)

        @pl.when(h == home)
        def keep():
            rbuf[home] = moved

        @pl.when(h != home)
        def send():
            comp[h] = moved
            post(h).start()

    state = [jnp.concatenate([eye_f, zero], axis=1) for h in range(heads)]
    for b in range(count):
        span = pl.ds(b * BLK, BLK)
        for h in range(heads):
            now = state[h]
            kb = kh[h, span, :].astype(BF16)
            rs = rsf[h, span, :]
            beta = btf[h, span, :]
            moved = dot2(kb, split(now))
            y = jnp.concatenate(
                [(-rs * beta) * moved[:, :HD], beta * (vh[h, span, :] - rs * moved[:, HD:])],
                axis=1,
            )
            d = dot3((invn[h, b, 0], invn[h, b, 1]), split(y))
            fa[h, 2 * b] = now[:, :HD]
            fb[h, 2 * b] = now[:, HD:]
            fa[h, 2 * b + 1] = d[:, :HD]
            fb[h, 2 * b + 1] = d[:, HD:]
            rs2 = jnp.concatenate([rs, rs], axis=1)
            state[h] = now + dot2(ktr[h, b], split(rs2 * d))
    for h in range(heads):
        mine[0, h] = state[h]

    @pl.when(back == 1)
    def hand_forward():
        for h in range(heads):
            hand_over(0, h).start()

    own_cot.wait()
    cot_copies[2].wait_recv()
    cot_copies[3].wait_recv()
    hand_right.wait_recv()
    hand_left.wait_recv()
    fetch_w.wait()
    width = cot_ref.shape[1]
    for n in range(heads // 2):
        acc = jnp.zeros((rows, 2 * HD), F32)
        for j in range(zsize):
            acc = acc + dg(
                full[j],
                wbuf[2 * n * HD : 2 * (n + 1) * HD, j * width : (j + 1) * width],
                NT,
            )
        for i in range(2):
            hi, lo = split(acc[:, i * HD : (i + 1) * HD])
            gsp[2 * n + i, 0] = hi
            gsp[2 * n + i, 1] = lo

    def pair_of(turn):
        return (lax.rem(home + 2 + turn, heads), lax.rem(home + 1 - turn + heads, heads))

    @pl.when(back == 0)
    def combine_forward():
        for turn in range(heads // 2):
            for h in pair_of(turn):
                combine(0, h)

    seen_t = (iota2((BLK, tokens), 0) // refl) <= iota2((BLK, tokens), 1)

    def backward(turn, carry):
        pair = pair_of(turn)
        state = [jnp.concatenate([eye_f, zero], axis=1) for h in pair]
        for b in reversed(range(count)):
            span = pl.ds(b * BLK, BLK)
            tspan = pl.ds(b * tokens, tokens)
            for i, h in enumerate(pair):
                now = state[i]
                kb = kh[h, span, :].astype(BF16)
                rs = rsf[h, span, :]
                beta = btf[h, span, :]
                qb = qh[h, tspan, :]
                gs = (gsp[h, 0, tspan, :], gsp[h, 1, tspan, :])
                sc_t = jnp.where(seen_t, dg(kb, qb, NT) * (rs[:, :tokens] * scale), 0.0)
                direct = dot3(split(sc_t), gs)
                moved = dot2(kb, split(now))
                dd = jnp.concatenate([rs * moved[:, :HD], rs * moved[:, HD:] + direct], axis=1)
                f = dot3((invt[h, b, 0], invt[h, b, 1]), split(dd))
                ba[h, 2 * b] = now[:, :HD]
                bb[h, 2 * b] = now[:, HD:]
                ba[h, 2 * b + 1] = f[:, :HD]
                bb[h, 2 * b + 1] = f[:, HD:]
                source = dot2(qb.T, gs) * scale
                rb = rs * beta
                rb2 = jnp.concatenate([rb, rb], axis=1)
                state[i] = (
                    now
                    + jnp.concatenate([zero, source], axis=1)
                    - dot2(ktr[h, b], split(rb2 * f))
                )
        for i, h in enumerate(pair):
            mine[1, h] = state[i]

        @pl.when(back == 0)
        def hand_backward():
            for h in pair:
                hand_over(1, h).start()

        @pl.when((back == 1) & (turn == 1))
        def combine_backward():
            for h in pair_of(0):
                combine(1, h)

        return carry

    lax.fori_loop(0, heads // 2, backward, 0)

    @pl.when(back == 1)
    def combine_last():
        for h in pair_of(1):
            combine(1, h)

    total[:, :HD] = eye_f
    total[:, HD:] = zero

    def advance(step, carry):
        source = step + back * (heads - 1 - 2 * step)

        @pl.when(source != home)
        def wait_other():
            remote(
                comp.at[source], rbuf.at[source], comp_send.at[source], comp_recv.at[source],
                seq=chip(source),
            ).wait_recv()

        now = total[...]
        pref[source] = now
        moved = dot3(split(rbuf[source, :, :HD]), split(now))
        total[:, :HD] = moved[:, :HD]
        total[:, HD:] = moved[:, HD:] + rbuf[source, :, HD:]
        return carry

    lax.fori_loop(0, heads, advance, 0)

    def chain(r, slot):
        return remote(chain_out, entry_in, chain_send.at[slot], chain_recv, seq=at_rank(r))

    def chain_map():
        return remote(total, ahead_map, chain_send.at[0], map_recv, seq=at_rank(3))

    @pl.when(rank == 0)
    def begin_chain():
        chain_out[...] = total[:, HD:]
        chain(1, 0).start()
        entry_in[...] = zero

    @pl.when(rank == 2)
    def offer_map():
        chain_map().start()

    seen = (iota2((tokens, BLK), 1) // refl) <= iota2((tokens, BLK), 0)

    def visit(turn):
        return lax.rem(home + turn + (turn // 2) * (1 - 2 * lax.rem(turn, 2)), heads)

    def give(x):
        return remote(
            entries.at[x], both.at[back, home], ent_send.at[x], ent_recv.at[home], seq=chip(x)
        )

    def tell(h):
        return remote(
            entries.at[heads + h], both.at[back, h], oth_send.at[h], oth_recv.at[h], seq=partner
        )

    def told(h):
        remote(
            entries.at[heads + h], both.at[1 - back, h], oth_send.at[h], oth_recv.at[h],
            seq=partner,
        ).wait_recv()

    def relay(turn):
        h = visit(turn)

        @pl.when(h != home)
        def take():
            remote(
                entries.at[h], both.at[back, h], ent_send.at[h], ent_recv.at[h], seq=chip(h)
            ).wait_recv()

        entries[heads + h] = (
            dot3(split(mine[back, h, :, :HD]), split(both[back, h])) + mine[back, h, :, HD:]
        )
        tell(h).start()

    deep = 2 * count * BLK

    def first_part(turn, carry):
        h = visit(turn)

        @pl.when((back == 0) & (turn + 1 < heads))
        def look_ahead():
            relay(turn + 1)

        @pl.when(back == 1)
        def listen():
            told(h)

        begin = split(both[0, h])
        sd = dot3(split(fa[h].reshape(deep, HD)), begin) + fb[h].reshape(deep, HD)
        fb[h] = sd.reshape(2 * count, BLK, HD)
        for b in range(count):
            span = pl.ds(b * BLK, BLK)
            tspan = pl.ds(b * tokens, tokens)
            kb = kh[h, span, :].astype(BF16)
            rs_row = to_row(rsf[h, span, :], eye)
            at = 2 * b * BLK
            ds, ss = split(sd[at + BLK : at + 2 * BLK]), split(sd[at : at + BLK])
            gs = (gsp[h, 0, tspan, :], gsp[h, 1, tspan, :])
            dsc = jnp.where(seen, dot3t(gs, ds), 0.0)
            qg_ref[pl.ds(b * tokens * heads + h, tokens, stride=heads), :] = scale * (
                dot3t(gs, ss) + dot2l(split(dsc * rs_row), kb)
            )
            vh[h, span, :] = dot2l(split(dsc.T * scale), qh[h, tspan, :])
        return carry

    early = (back == 1) & (line <= 1)

    @pl.when(early)
    def first_early():
        lax.fori_loop(0, heads, first_part, 0)

    @pl.when(rank != 0)
    def await_chain():
        chain(1, 0).wait_recv()

    @pl.when(rank == 1)
    def pass_on():
        chain_out[...] = dot3(split(total[:, :HD]), split(entry_in[...])) + total[:, HD:]
        chain(3, 1).start()
        chain(2, 0).start()

    @pl.when(rank == 3)
    def skip_one():
        chain_map().wait_recv()
        entry_in[...] = (
            dot3(split(ahead_map[:, :HD]), split(entry_in[...])) + ahead_map[:, HD:]
        )

    states = split(entry_in[...])
    both[back, home] = dot3(split(pref[home, :, :HD]), states) + pref[home, :, HD:]
    relay(0)

    def finish(step, carry):
        x = lax.rem(home + step, heads)
        entries[x] = dot3(split(pref[x, :, :HD]), states) + pref[x, :, HD:]
        give(x).start()
        return carry

    lax.fori_loop(1, heads, finish, 0)

    @pl.when(jnp.logical_not(early))
    def first_late():
        lax.fori_loop(0, heads, first_part, 0)

    def second_part(turn, carry):
        h = visit(turn)

        @pl.when((back == 1) & (turn + 1 < heads))
        def look_ahead():
            relay(turn + 1)

        @pl.when(back == 0)
        def listen():
            told(h)

        final = split(both[1, h])
        lf = dot3(split(ba[h].reshape(deep, HD)), final) + bb[h].reshape(deep, HD)
        acc = jnp.zeros((8, rows), F32)
        for b in range(count):
            span = pl.ds(b * BLK, BLK)
            kf = kh[h, span, :]
            kt = ktr[h, b]
            rs = rsf[h, span, :]
            beta = btf[h, span, :]
            rs_row = to_row(rs, eye)
            at = 2 * b * BLK
            s0, delta = fb[h, 2 * b], fb[h, 2 * b + 1]
            lam, f = lf[at : at + BLK], lf[at + BLK : at + 2 * BLK]
            e = beta * f
            dlog = jnp.sum(f * delta, axis=1, keepdims=True) * (1.0 - 0.5 * beta)
            dlog = jnp.where(col == row // refl + b * tokens, dlog, 0.0)
            for i in range(BLK // 8):
                acc = acc + dlog[8 * i : 8 * (i + 1), :]
            wide[pl.ds(b * BLK, BLK), :] = e
            ds, es, ss, ls = split(delta), split(e), split(s0), split(lam)
            m = jnp.where(col < row, dot3t(es, ds), 0.0)
            ms = split((m + m.T) * rs_row)
            dk = dg(
                jnp.concatenate([ds[0], ds[1], ds[0]], 1),
                jnp.concatenate([ls[0], ls[0], ls[1]], 1),
                NT,
            ) - dg(
                jnp.concatenate([es[0], es[1], es[0], ms[0], ms[1]], 1),
                jnp.concatenate([ss[0], ss[0], ss[1], kt, kt], 1),
                NT,
            )
            dk = dk + vh[h, span, :]
            ku = kf * rs
            along = jnp.sum(ku * dk, axis=1, keepdims=True)
            wide[pl.ds((count + b) * BLK, BLK), :] = rs * (dk - ku * along)
        for r in range(refl):
            lane = pl.ds(h * refl + r, rows, stride=per_token)
            vg_ref[lane, :] = wide[pl.ds(r, rows, stride=refl), :]
            kg_ref[lane, :] = wide[pl.ds(steps + r, rows, stride=refl), :]
        out = acc[:refl]
        for i in range(1, 8 // refl):
            out = out + acc[i * refl : (i + 1) * refl]
        lgg_ref[h] = out
        return carry

    lax.fori_loop(0, heads, second_part, 0)

    for copy in cot_copies:
        copy.wait_send()
    hand_right.wait_send()
    hand_left.wait_send()
    for h in range(heads):
        hand_over(0, h).wait_send()
        tell(h).wait_send()

    def drain(step, carry):
        x = lax.rem(home + step, heads)
        post(x).wait_send()
        give(x).wait_send()
        return carry

    lax.fori_loop(1, heads, drain, 0)

    @pl.when(rank <= 1)
    def sent_on():
        chain(1, 0).wait_send()

    @pl.when(rank == 1)
    def sent_both():
        chain(3, 1).wait_send()

    @pl.when(rank == 2)
    def sent_map():
        chain_map().wait_send()


def layer(q, k, v, lg, cot, w):
    heads, refl, rows = lg.shape
    steps = rows * refl
    count = steps // BLK
    zsize = lax.axis_size("head")
    dma = pltpu.SemaphoreType.DMA
    vm = pl.BlockSpec(memory_space=pltpu.VMEM)
    saved = pltpu.VMEM((heads, 2 * count, BLK, HD), F32)
    many = pltpu.VMEM((heads, steps, HD), F32)
    aug = pltpu.VMEM((heads, HD, 2 * HD), F32)
    return pl.pallas_call(
        layer_kernel,
        out_shape=(
            jax.ShapeDtypeStruct(q.shape, F32),
            jax.ShapeDtypeStruct(k.shape, F32),
            jax.ShapeDtypeStruct(v.shape, F32),
            jax.ShapeDtypeStruct(lg.shape, F32),
        ),
        in_specs=[vm] * 5 + [pl.BlockSpec(memory_space=pl.ANY)],
        out_specs=(vm,) * 4,
        scratch_shapes=[
            pltpu.VMEM(k.shape, F32),
            many,
            pltpu.VMEM((heads, count, HD, BLK), BF16),
            many,
            pltpu.VMEM((heads, rows, HD), BF16),
            many,
            many,
            pltpu.VMEM((heads, count, 2, BLK, BLK), BF16),
            pltpu.VMEM((heads, count, 2, BLK, BLK), BF16),
            pltpu.VMEM((heads, 2, rows, HD), BF16),
            saved, saved, saved, saved,
            pltpu.VMEM((zsize,) + cot.shape, BF16),
            pltpu.VMEM(w.shape, BF16),
            pltpu.VMEM((2, heads, HD, 2 * HD), F32),
            aug, aug, aug, aug,
            pltpu.VMEM((HD, 2 * HD), F32),
            pltpu.VMEM((HD, HD), F32),
            pltpu.VMEM((HD, 2 * HD), F32),
            pltpu.VMEM((HD, HD), F32),
            pltpu.VMEM((2 * heads, HD, HD), F32),
            pltpu.VMEM((2, heads, HD, HD), F32),
            dma, dma, dma((6,)), dma((6,)),
            dma((heads,)), dma((heads,)), dma((heads,)), dma((heads,)),
            dma((2,)), dma, dma,
            dma((heads,)), dma((heads,)), dma((heads,)), dma((heads,)),
        ],
        compiler_params=pltpu.CompilerParams(collective_id=0, has_side_effects=True),
        name="layer",
    )(q, k, v, lg, cot, w)


def emit_kernel(*refs):
    half = len(refs) // 2
    for source, target in zip(refs[:half], refs[half:]):
        target[...] = source[...]


def emit(q, k, v, lg):
    parts = 4
    specs = [pl.BlockSpec((x.shape[0] // parts,) + x.shape[1:], lambda i: (i, 0)) for x in (q, k, v)]
    specs.append(pl.BlockSpec((lg.shape[0] // parts,) + lg.shape[1:], lambda i: (i, 0, 0)))
    return pl.pallas_call(
        emit_kernel,
        grid=(parts,),
        out_shape=[jax.ShapeDtypeStruct(x.shape, x.dtype) for x in (q, k, v, lg)],
        in_specs=specs,
        out_specs=specs,
        name="emit",
    )(q, k, v, lg)


def local(queries, keys, values, beta_logits, out_cot, out_weight):
    rows, heads, width = queries.shape
    refl = keys.shape[2]
    results = layer(
        queries.reshape(rows * heads, width),
        keys.reshape(rows * heads * refl, width),
        values.reshape(rows * heads * refl, width),
        beta_logits,
        out_cot,
        out_weight,
    )
    query_grad, key_grad, value_grad, beta_grad = emit(*results)
    return (
        query_grad.reshape(queries.shape),
        key_grad.reshape(keys.shape),
        value_grad.reshape(values.shape),
        beta_grad,
    )


def solution(mesh):
    return jax.shard_map(
        local,
        mesh=mesh,
        in_specs=(
            P("seq", "head", None),
            P("seq", "head", None, None),
            P("seq", "head", None, None),
            P("head", None, "seq"),
            P("seq", "head"),
            P("head", None),
        ),
        out_specs=(
            P("seq", "head", None),
            P("seq", "head", None, None),
            P("seq", "head", None, None),
            P("head", None, "seq"),
        ),
        check_vma=False,
    )
```

```python
import jax
import jax.numpy as jnp
from jax import lax
from jax.experimental import pallas as pl
from jax.experimental.pallas import tpu as pltpu
from jax.sharding import PartitionSpec as P

F32 = jnp.float32
BF16 = jnp.bfloat16
MESH = pl.DeviceIdType.MESH
HD = 128
BLK = 128
NT = (((1,), (1,)), ((), ()))
NN = (((1,), (0,)), ((), ()))


def dg(a, b, dims):
    return lax.dot_general(a, b, dims, preferred_element_type=F32)


def split(x):
    hi = x.astype(BF16)
    lo = (x - hi.astype(F32)).astype(BF16)
    return hi, lo


def dot2(a, bs):
    return dg(jnp.concatenate([a, a], 1), jnp.concatenate(bs, 0), NN)


def dot2l(as_, b):
    return dg(jnp.concatenate(as_, 1), jnp.concatenate([b, b], 0), NN)


def dot3(as_, bs):
    left = jnp.concatenate([as_[0], as_[1], as_[0]], 1)
    right = jnp.concatenate([bs[0], bs[0], bs[1]], 0)
    return dg(left, right, NN)


def dot3t(as_, bs):
    left = jnp.concatenate([as_[0], as_[1], as_[0]], 1)
    right = jnp.concatenate([bs[0], bs[0], bs[1]], 1)
    return dg(left, right, NT)


def iota2(shape, axis):
    return lax.broadcasted_iota(jnp.int32, shape, axis)


def to_row(full, eye):
    return jnp.sum(jnp.where(eye, full, 0.0), axis=0, keepdims=True)


def remote(src, dst, send, recv, **device):
    return pltpu.make_async_remote_copy(
        src_ref=src,
        dst_ref=dst,
        send_sem=send,
        recv_sem=recv,
        device_id=device,
        device_id_type=MESH,
    )


def diagonal_inverse(lower, small, row, col, spread):
    units = len(lower)
    packed = []
    band = col[:small] // small
    for n in lower:
        acc = jnp.where(band == 0, n[:small], 0.0)
        for i in range(1, BLK // small):
            acc = jnp.where(band == i, n[i * small : (i + 1) * small], acc)
        packed.append(acc)
    hi, lo = split(jnp.concatenate(packed, 0))
    both = jnp.concatenate([hi, lo], 1)
    unit = jnp.where(row[:small] == col[:small] % small, 1.0, 0.0)
    xs = [unit] * units
    for j in range(small - 1):
        factor = dg(both, spread[j], NN)
        for u in range(units):
            xs[u] = xs[u] - factor[u * small : (u + 1) * small] * xs[u][j : j + 1]
    return [
        jnp.concatenate([jnp.where(band == i, x, 0.0) for i in range(BLK // small)], 0)
        for x in xs
    ]


def grow_inverse(inv, lower, s, row, col):
    mask = ((row // (2 * s)) == (col // (2 * s))) & ((col // s) % 2 == 0)
    odds = [slice(i, i + s) for i in range(s, BLK, 2 * s)]
    grown = []
    for x, n in zip(inv, lower):
        cut = jnp.where(mask, n, 0.0)
        below = jnp.concatenate([cut[o] for o in odds], 0)
        y = dot3(split(below), split(x))
        gap = jnp.zeros((s, BLK), F32)
        parts = []
        for i in range(len(odds)):
            parts += [gap, y[i * s : (i + 1) * s]]
        odd = jnp.concatenate([x[o] for o in odds], 0)
        new = odd - dot3(split(odd), split(jnp.concatenate(parts, 0)))
        parts = []
        for i, o in enumerate(odds):
            parts += [x[o.start - s : o.start], new[i * s : (i + 1) * s]]
        grown.append(jnp.concatenate(parts, 0))
    return grown


def layer_kernel(q_ref, k_ref, v_ref, lg_ref, cot_ref, w_ref,
                 qg_ref, kg_ref, vg_ref, lgg_ref,
                 wide, kh, khb, kns, knt, vh, qh, rsf, btf, invn, invt, gsp, fa, fb, ba, bb,
                 full, wbuf, mine, pm, comp, rbuf, pref, total, entry_in, ahead_map, chain_out,
                 entries, both,
                 w_sem, cot_own, cot_send, cot_recv, pm_send, pm_recv, comp_send, comp_recv,
                 chain_send, chain_recv, map_recv, ent_send, ent_recv, oth_send, oth_recv):
    heads, refl, rows = lg_ref.shape
    steps = rows * refl
    count = steps // BLK
    tokens = rows // count
    scale = HD ** (-0.5)
    lanes = 2 * heads
    zsize = lax.axis_size("head")
    lines = lax.axis_size("seq") // lanes
    zme = lax.axis_index("head")
    index = lax.axis_index("seq")
    line = index // lanes
    me = lax.rem(index, lanes)
    back = lax.rem(me, 2)
    home = me // 2
    partner = index + 1 - 2 * back
    rank = line + back * (lines - 1 - 2 * line)

    def chip(x):
        return line * lanes + 2 * x + back

    def at_rank(r):
        return (r + back * (lines - 1 - 2 * r)) * lanes + me

    fetch_w = pltpu.make_async_copy(w_ref, wbuf, w_sem)
    fetch_w.start()
    barrier = pltpu.get_barrier_semaphore()
    zright = lax.rem(zme + 1, zsize)
    zleft = lax.rem(zme + zsize - 1, zsize)
    for peer in (zright, zleft):
        pl.semaphore_signal(barrier, inc=1, device_id={"head": peer}, device_id_type=MESH)
    friends = [partner]
    friends += [chip(lax.rem(home + step, heads)) for step in range(1, heads)]
    friends += [lax.rem(line + step, lines) * lanes + me for step in range(1, lines)]
    for peer in friends:
        pl.semaphore_signal(barrier, inc=1, device_id={"seq": peer}, device_id_type=MESH)

    per_token = heads * refl
    wide[...] = k_ref[...].astype(F32)
    for h in range(heads):
        for r in range(refl):
            kh[h, pl.ds(r, rows, stride=refl), :] = wide[
                pl.ds(h * refl + r, rows, stride=per_token), :
            ]

    half = rows // 2
    low, high = pl.ds(0, half), pl.ds(half, half)
    cot_copies = [
        remote(cot_ref.at[low], full.at[zme, low], cot_send.at[0], cot_recv.at[0], head=zright),
        remote(cot_ref.at[high], full.at[zme, high], cot_send.at[1], cot_recv.at[1], head=zleft),
        remote(cot_ref.at[high], full.at[zme, high], cot_send.at[2], cot_recv.at[2], head=zright),
        remote(cot_ref.at[low], full.at[zme, low], cot_send.at[3], cot_recv.at[3], head=zleft),
    ]
    own_cot = pltpu.make_async_copy(cot_ref, full.at[zme], cot_own)
    own_cot.start()
    hand_right = remote(
        full.at[zleft, low], full.at[zleft, low], cot_send.at[4], cot_recv.at[4], head=zright
    )
    hand_left = remote(
        full.at[zright, high], full.at[zright, high], cot_send.at[5], cot_recv.at[5], head=zleft
    )

    wide[...] = v_ref[...].astype(F32)
    for h in range(heads):
        for r in range(refl):
            vh[h, pl.ds(r, rows, stride=refl), :] = wide[
                pl.ds(h * refl + r, rows, stride=per_token), :
            ]
    wide[pl.ds(0, rows * heads), :] = q_ref[...].astype(F32)
    for h in range(heads):
        qh[h] = wide[pl.ds(h, rows, stride=heads), :].astype(BF16)

    row = iota2((BLK, BLK), 0)
    col = iota2((BLK, BLK), 1)
    eye = row == col
    eye_f = jnp.where(eye, 1.0, 0.0)
    zero = jnp.zeros((BLK, HD), F32)
    small = 16

    def invert(turn, carry):
        @pl.when(turn == 1)
        def greet():
            pl.semaphore_wait(barrier, 2 + len(friends))
            for copy in cot_copies:
                copy.start()

        units = [(2 * turn + i, b) for b in range(count) for i in range(2)]
        lower, strengths = [], []
        for h, b in units:
            span = pl.ds(b * BLK, BLK)
            kf = kh[h, span, :]
            kb = kf.astype(BF16)
            rs = lax.rsqrt(jnp.sum(kf * kf, axis=1, keepdims=True) + 1e-06)
            beta4 = 2.0 / (1.0 + jnp.exp(-lg_ref[h]))
            beta_all = jnp.tile(jnp.concatenate([beta4] * (8 // refl), 0), (BLK // 8, 1))
            beta = jnp.sum(
                jnp.where(col == row // refl + b * tokens, beta_all, 0.0), axis=1, keepdims=True
            )
            rs = jnp.broadcast_to(rs, (BLK, HD))
            beta = jnp.broadcast_to(beta, (BLK, HD))
            rsf[h, span, :] = rs
            btf[h, span, :] = 1.0 / beta - 0.5
            strengths.append(to_row(beta, eye))
            kn = kf * rs
            kh[h, span, :] = kn
            khb[h, span, :] = kb
            for part, x in enumerate(split(kn)):
                kns[h, b, part] = x
                knt[h, b, part] = x.T
            n = jnp.where(col < row, dg(kb, kb, NT) * (rs * beta) * to_row(rs, eye), 0.0)
            lower.append(n)
        spread = []
        for j in range(small - 1):
            pick = jnp.where(row == (col // small) * small + j, 1.0, 0.0).astype(BF16)
            spread.append(jnp.concatenate([pick, pick], 0))
        inv = diagonal_inverse(lower, small, row, col, spread)
        s = small
        while s < BLK:
            inv = grow_inverse(inv, lower, s, row, col)
            s *= 2
        for (h, b), x, strength in zip(units, inv, strengths):
            hi, lo = split(x * strength)
            invn[h, b, 0] = hi
            invn[h, b, 1] = lo
            invt[h, b, 0] = hi.T
            invt[h, b, 1] = lo.T
        return carry

    lax.fori_loop(0, heads // 2, invert, 0)
    cot_copies[0].wait_recv()
    hand_right.start()
    cot_copies[1].wait_recv()
    hand_left.start()

    def hand_over(direction, h):
        return remote(mine.at[direction, h], pm.at[h], pm_send.at[h], pm_recv.at[h], seq=partner)

    def post(h):
        return remote(
            comp.at[h], rbuf.at[home], comp_send.at[h], comp_recv.at[home], seq=chip(h)
        )

    def combine(direction, h):
        hand_over(direction, h).wait_recv()
        moved = dot3(split(pm[h, :, :HD]), split(mine[direction, h]))
        moved = jnp.concatenate([moved[:, :HD], moved[:, HD:] + pm[h, :, HD:]], axis=1)

        @pl.when(h == home)
        def keep():
            rbuf[home] = moved

        @pl.when(h != home)
        def send():
            comp[h] = moved
            post(h).start()

    state = [jnp.concatenate([eye_f, zero], axis=1) for h in range(heads)]
    for b in range(count):
        span = pl.ds(b * BLK, BLK)
        for h in range(heads):
            now = state[h]
            vb = vh[h, span, :]
            if b == 0:
                y = jnp.concatenate([-kh[h, span, :], vb], axis=1)
            else:
                moved = dot3((kns[h, b, 0], kns[h, b, 1]), split(now))
                y = jnp.concatenate([-moved[:, :HD], vb - moved[:, HD:]], axis=1)
            d = dot3((invn[h, b, 0], invn[h, b, 1]), split(y))
            fa[h, 2 * b] = now[:, :HD]
            fb[h, 2 * b] = now[:, HD:]
            fa[h, 2 * b + 1] = d[:, :HD]
            fb[h, 2 * b + 1] = d[:, HD:]
            state[h] = now + dot3((knt[h, b, 0], knt[h, b, 1]), split(d))
    for h in range(heads):
        mine[0, h] = state[h]

    @pl.when(back == 1)
    def hand_forward():
        for h in range(heads):
            hand_over(0, h).start()

    own_cot.wait()
    cot_copies[2].wait_recv()
    cot_copies[3].wait_recv()
    hand_right.wait_recv()
    hand_left.wait_recv()
    fetch_w.wait()
    width = cot_ref.shape[1]
    for n in range(heads // 2):
        acc = jnp.zeros((rows, 2 * HD), F32)
        for j in range(zsize):
            acc = acc + dg(
                full[j],
                wbuf[2 * n * HD : 2 * (n + 1) * HD, j * width : (j + 1) * width],
                NT,
            )
        for i in range(2):
            hi, lo = split(acc[:, i * HD : (i + 1) * HD])
            gsp[2 * n + i, 0] = hi
            gsp[2 * n + i, 1] = lo

    def pair_of(turn):
        return (lax.rem(home + 2 + turn, heads), lax.rem(home + 1 - turn + heads, heads))

    @pl.when(back == 0)
    def combine_forward():
        for turn in range(heads // 2):
            for h in pair_of(turn):
                combine(0, h)

    seen_t = (iota2((BLK, tokens), 0) // refl) <= iota2((BLK, tokens), 1)

    def backward(turn, carry):
        pair = pair_of(turn)
        state = [jnp.concatenate([eye_f, zero], axis=1) for h in pair]
        for b in reversed(range(count)):
            span = pl.ds(b * BLK, BLK)
            tspan = pl.ds(b * tokens, tokens)
            for i, h in enumerate(pair):
                now = state[i]
                kb = khb[h, span, :]
                rs = rsf[h, span, :]
                qb = qh[h, tspan, :]
                gs = (gsp[h, 0, tspan, :], gsp[h, 1, tspan, :])
                sc_t = jnp.where(seen_t, dg(kb, qb, NT) * (rs[:, :tokens] * scale), 0.0)
                direct = dot3(split(sc_t), gs)
                if b == count - 1:
                    dd = jnp.concatenate([kh[h, span, :], direct], axis=1)
                else:
                    moved = dot3((kns[h, b, 0], kns[h, b, 1]), split(now))
                    dd = jnp.concatenate([moved[:, :HD], moved[:, HD:] + direct], axis=1)
                f = dot3((invt[h, b, 0], invt[h, b, 1]), split(dd))
                ba[h, 2 * b] = now[:, :HD]
                bb[h, 2 * b] = now[:, HD:]
                ba[h, 2 * b + 1] = f[:, :HD]
                bb[h, 2 * b + 1] = f[:, HD:]
                source = dot2(qb.T, gs) * scale
                state[i] = (
                    now
                    + jnp.concatenate([zero, source], axis=1)
                    - dot3((knt[h, b, 0], knt[h, b, 1]), split(f))
                )
        for i, h in enumerate(pair):
            mine[1, h] = state[i]

        @pl.when(back == 0)
        def hand_backward():
            for h in pair:
                hand_over(1, h).start()

        @pl.when((back == 1) & (turn == 1))
        def combine_backward():
            for h in pair_of(0):
                combine(1, h)

        return carry

    lax.fori_loop(0, heads // 2, backward, 0)

    @pl.when(back == 1)
    def combine_last():
        for h in pair_of(1):
            combine(1, h)

    total[:, :HD] = eye_f
    total[:, HD:] = zero

    def advance(step, carry):
        source = step + back * (heads - 1 - 2 * step)

        @pl.when(source != home)
        def wait_other():
            remote(
                comp.at[source], rbuf.at[source], comp_send.at[source], comp_recv.at[source],
                seq=chip(source),
            ).wait_recv()

        now = total[...]
        pref[source] = now
        moved = dot3(split(rbuf[source, :, :HD]), split(now))
        total[:, :HD] = moved[:, :HD]
        total[:, HD:] = moved[:, HD:] + rbuf[source, :, HD:]
        return carry

    lax.fori_loop(0, heads, advance, 0)

    def chain(r, slot):
        return remote(chain_out, entry_in, chain_send.at[slot], chain_recv, seq=at_rank(r))

    def chain_map():
        return remote(total, ahead_map, chain_send.at[0], map_recv, seq=at_rank(3))

    @pl.when(rank == 0)
    def begin_chain():
        chain_out[...] = total[:, HD:]
        chain(1, 0).start()
        entry_in[...] = zero

    @pl.when(rank == 2)
    def offer_map():
        chain_map().start()

    seen = (iota2((tokens, BLK), 1) // refl) <= iota2((tokens, BLK), 0)

    def visit(turn):
        return lax.rem(home + turn + (turn // 2) * (1 - 2 * lax.rem(turn, 2)), heads)

    def give(x):
        return remote(
            entries.at[x], both.at[back, home], ent_send.at[x], ent_recv.at[home], seq=chip(x)
        )

    def tell(h):
        return remote(
            entries.at[heads + h], both.at[back, h], oth_send.at[h], oth_recv.at[h], seq=partner
        )

    def told(h):
        remote(
            entries.at[heads + h], both.at[1 - back, h], oth_send.at[h], oth_recv.at[h],
            seq=partner,
        ).wait_recv()

    def relay(turn):
        h = visit(turn)

        @pl.when(h != home)
        def take():
            remote(
                entries.at[h], both.at[back, h], ent_send.at[h], ent_recv.at[h], seq=chip(h)
            ).wait_recv()

        entries[heads + h] = (
            dot3(split(mine[back, h, :, :HD]), split(both[back, h])) + mine[back, h, :, HD:]
        )
        tell(h).start()

    deep = 2 * count * BLK

    def first_part(turn, carry):
        h = visit(turn)

        @pl.when((back == 0) & (turn + 1 < heads))
        def look_ahead():
            relay(turn + 1)

        @pl.when(back == 1)
        def listen():
            told(h)

        begin = split(both[0, h])
        sd = dot3(split(fa[h].reshape(deep, HD)), begin) + fb[h].reshape(deep, HD)
        fb[h] = sd.reshape(2 * count, BLK, HD)
        for b in range(count):
            span = pl.ds(b * BLK, BLK)
            tspan = pl.ds(b * tokens, tokens)
            at = 2 * b * BLK
            ds, ss = split(sd[at + BLK : at + 2 * BLK]), split(sd[at : at + BLK])
            gs = (gsp[h, 0, tspan, :], gsp[h, 1, tspan, :])
            dsc = jnp.where(seen, dot3t(gs, ds), 0.0)
            qg_ref[pl.ds(b * tokens * heads + h, tokens, stride=heads), :] = scale * (
                dot3t(gs, ss) + dot3(split(dsc), (kns[h, b, 0], kns[h, b, 1]))
            )
            vh[h, span, :] = dot2l(split(dsc.T * scale), qh[h, tspan, :])
        return carry

    early = (back == 1) & (line <= 1)

    @pl.when(early)
    def first_early():
        lax.fori_loop(0, heads, first_part, 0)

    @pl.when(rank != 0)
    def await_chain():
        chain(1, 0).wait_recv()

    @pl.when(rank == 1)
    def pass_on():
        chain_out[...] = dot3(split(total[:, :HD]), split(entry_in[...])) + total[:, HD:]
        chain(3, 1).start()
        chain(2, 0).start()

    @pl.when(rank == 3)
    def skip_one():
        chain_map().wait_recv()
        entry_in[...] = (
            dot3(split(ahead_map[:, :HD]), split(entry_in[...])) + ahead_map[:, HD:]
        )

    states = split(entry_in[...])
    both[back, home] = dot3(split(pref[home, :, :HD]), states) + pref[home, :, HD:]
    relay(0)

    def finish(step, carry):
        x = lax.rem(home + step, heads)
        entries[x] = dot3(split(pref[x, :, :HD]), states) + pref[x, :, HD:]
        give(x).start()
        return carry

    lax.fori_loop(1, heads, finish, 0)

    @pl.when(jnp.logical_not(early))
    def first_late():
        lax.fori_loop(0, heads, first_part, 0)

    def second_part(turn, carry):
        h = visit(turn)

        @pl.when((back == 1) & (turn + 1 < heads))
        def look_ahead():
            relay(turn + 1)

        @pl.when(back == 0)
        def listen():
            told(h)

        final = split(both[1, h])
        lf = dot3(split(ba[h].reshape(deep, HD)), final) + bb[h].reshape(deep, HD)
        acc = jnp.zeros((8, rows), F32)
        for b in range(count):
            span = pl.ds(b * BLK, BLK)
            ku = kh[h, span, :]
            kt = (knt[h, b, 0], knt[h, b, 1])
            rs = rsf[h, span, :]
            at = 2 * b * BLK
            s0, delta = fb[h, 2 * b], fb[h, 2 * b + 1]
            lam, e = lf[at : at + BLK], lf[at + BLK : at + 2 * BLK]
            dlog = jnp.sum(e * delta, axis=1, keepdims=True) * btf[h, span, :]
            dlog = jnp.where(col == row // refl + b * tokens, dlog, 0.0)
            for i in range(BLK // 8):
                acc = acc + dlog[8 * i : 8 * (i + 1), :]
            wide[pl.ds(b * BLK, BLK), :] = e
            ds, es, ss, ls = split(delta), split(e), split(s0), split(lam)
            m = jnp.where(col < row, dot3t(es, ds), 0.0)
            ms = split(m + m.T)
            dk = dg(
                jnp.concatenate([ds[0], ds[1], ds[0]], 1),
                jnp.concatenate([ls[0], ls[0], ls[1]], 1),
                NT,
            ) - dg(
                jnp.concatenate([es[0], es[1], es[0], ms[0], ms[1], ms[0]], 1),
                jnp.concatenate([ss[0], ss[0], ss[1], kt[0], kt[0], kt[1]], 1),
                NT,
            )
            dk = dk + vh[h, span, :]
            along = jnp.sum(ku * dk, axis=1, keepdims=True)
            wide[pl.ds((count + b) * BLK, BLK), :] = rs * (dk - ku * along)
        for r in range(refl):
            lane = pl.ds(h * refl + r, rows, stride=per_token)
            vg_ref[lane, :] = wide[pl.ds(r, rows, stride=refl), :]
            kg_ref[lane, :] = wide[pl.ds(steps + r, rows, stride=refl), :]
        out = acc[:refl]
        for i in range(1, 8 // refl):
            out = out + acc[i * refl : (i + 1) * refl]
        lgg_ref[h] = out
        return carry

    lax.fori_loop(0, heads, second_part, 0)

    for copy in cot_copies:
        copy.wait_send()
    hand_right.wait_send()
    hand_left.wait_send()
    for h in range(heads):
        hand_over(0, h).wait_send()
        tell(h).wait_send()

    def drain(step, carry):
        x = lax.rem(home + step, heads)
        post(x).wait_send()
        give(x).wait_send()
        return carry

    lax.fori_loop(1, heads, drain, 0)

    @pl.when(rank <= 1)
    def sent_on():
        chain(1, 0).wait_send()

    @pl.when(rank == 1)
    def sent_both():
        chain(3, 1).wait_send()

    @pl.when(rank == 2)
    def sent_map():
        chain_map().wait_send()


def layer(q, k, v, lg, cot, w):
    heads, refl, rows = lg.shape
    steps = rows * refl
    count = steps // BLK
    zsize = lax.axis_size("head")
    dma = pltpu.SemaphoreType.DMA
    vm = pl.BlockSpec(memory_space=pltpu.VMEM)
    saved = pltpu.VMEM((heads, 2 * count, BLK, HD), F32)
    many = pltpu.VMEM((heads, steps, HD), F32)
    aug = pltpu.VMEM((heads, HD, 2 * HD), F32)
    return pl.pallas_call(
        layer_kernel,
        out_shape=(
            jax.ShapeDtypeStruct(q.shape, F32),
            jax.ShapeDtypeStruct(k.shape, F32),
            jax.ShapeDtypeStruct(v.shape, F32),
            jax.ShapeDtypeStruct(lg.shape, F32),
        ),
        in_specs=[vm] * 5 + [pl.BlockSpec(memory_space=pl.ANY)],
        out_specs=(vm,) * 4,
        scratch_shapes=[
            pltpu.VMEM(k.shape, F32),
            many,
            pltpu.VMEM((heads, steps, HD), BF16),
            pltpu.VMEM((heads, count, 2, BLK, HD), BF16),
            pltpu.VMEM((heads, count, 2, HD, BLK), BF16),
            many,
            pltpu.VMEM((heads, rows, HD), BF16),
            many,
            many,
            pltpu.VMEM((heads, count, 2, BLK, BLK), BF16),
            pltpu.VMEM((heads, count, 2, BLK, BLK), BF16),
            pltpu.VMEM((heads, 2, rows, HD), BF16),
            saved, saved, saved, saved,
            pltpu.VMEM((zsize,) + cot.shape, BF16),
            pltpu.VMEM(w.shape, BF16),
            pltpu.VMEM((2, heads, HD, 2 * HD), F32),
            aug, aug, aug, aug,
            pltpu.VMEM((HD, 2 * HD), F32),
            pltpu.VMEM((HD, HD), F32),
            pltpu.VMEM((HD, 2 * HD), F32),
            pltpu.VMEM((HD, HD), F32),
            pltpu.VMEM((2 * heads, HD, HD), F32),
            pltpu.VMEM((2, heads, HD, HD), F32),
            dma, dma, dma((6,)), dma((6,)),
            dma((heads,)), dma((heads,)), dma((heads,)), dma((heads,)),
            dma((2,)), dma, dma,
            dma((heads,)), dma((heads,)), dma((heads,)), dma((heads,)),
        ],
        compiler_params=pltpu.CompilerParams(collective_id=0, has_side_effects=True),
        name="layer",
    )(q, k, v, lg, cot, w)


def emit_kernel(*refs):
    count = (len(refs) - 2) // 3
    sources, targets, holds = refs[:count], refs[count : 2 * count], refs[2 * count : 3 * count]
    in_sem, out_sem = refs[3 * count :]
    parts = in_sem.shape[1]
    loads, stores = [], []
    for p in range(parts):
        for n in range(count):
            size = holds[n].shape[0] // parts
            span = pl.ds(p * size, size)
            loads.append(
                pltpu.make_async_copy(sources[n].at[span], holds[n].at[span], in_sem.at[n, p])
            )
            stores.append(
                pltpu.make_async_copy(holds[n].at[span], targets[n].at[span], out_sem.at[n, p])
            )
    for load in loads:
        load.start()
    for load, store in zip(loads, stores):
        load.wait()
        store.start()
    for store in stores:
        store.wait()


def emit(*arrays):
    parts = 4
    anywhere = pl.BlockSpec(memory_space=pl.ANY)
    return pl.pallas_call(
        emit_kernel,
        out_shape=[jax.ShapeDtypeStruct(x.shape, x.dtype) for x in arrays],
        in_specs=[anywhere] * len(arrays),
        out_specs=[anywhere] * len(arrays),
        scratch_shapes=[pltpu.VMEM(x.shape, x.dtype) for x in arrays]
        + [pltpu.SemaphoreType.DMA((len(arrays), parts))] * 2,
        name="emit",
    )(*arrays)


def local(queries, keys, values, beta_logits, out_cot, out_weight):
    rows, heads, width = queries.shape
    refl = keys.shape[2]
    results = layer(
        queries.reshape(rows * heads, width),
        keys.reshape(rows * heads * refl, width),
        values.reshape(rows * heads * refl, width),
        beta_logits,
        out_cot,
        out_weight,
    )
    query_grad, key_grad, value_grad, beta_grad = emit(*results)
    return (
        query_grad.reshape(queries.shape),
        key_grad.reshape(keys.shape),
        value_grad.reshape(values.shape),
        beta_grad,
    )


def solution(mesh):
    return jax.shard_map(
        local,
        mesh=mesh,
        in_specs=(
            P("seq", "head", None),
            P("seq", "head", None, None),
            P("seq", "head", None, None),
            P("head", None, "seq"),
            P("seq", "head"),
            P("head", None),
        ),
        out_specs=(
            P("seq", "head", None),
            P("seq", "head", None, None),
            P("seq", "head", None, None),
            P("head", None, "seq"),
        ),
        check_vma=False,
    )
```
